32 devices in a mesh: expert: 8 (over z, x), hidden: 4 (over y, core).
Axes of the slice: x: 2, y: 2, z: 4, core: 2. Of those that a mesh axis runs over, the one named last changes fastest.
Arguments:
- tokens: bfloat16 [1024, 4096], P('expert'), may hold values from -6 to 6
- cotangent: bfloat16 [1024, 4096], P('expert'), may hold values from -3 to 3
- expert_ids: int32 [1024, 2], P('expert'), may hold values from 0 to 7, as said below
- gate_codes: int32 [1024, 2], P('expert'), may hold values from 1 to 256
- up_weight: bfloat16 [8, 4096, 1024], P('expert', None, 'hidden'), may hold values from -0.09375 to 0.09375
- down_weight: bfloat16 [8, 1024, 4096], P('expert', 'hidden'), may hold values from -0.1875 to 0.1875
- threshold_state: int32 [8, 1024], P('expert', 'hidden'), may hold values from -64 to 191
- spike_mask: int32 [8, 1024], P('expert', 'hidden'), may hold values 0 or 1
Outputs:
- layer_out: bfloat16 [1024, 4096], P('expert', 'hidden')
- token_grad: bfloat16 [1024, 4096], P('expert', 'hidden')
- up_grad: bfloat16 [8, 4096, 1024], P('expert', None, 'hidden')
- down_grad: bfloat16 [8, 1024, 4096], P('expert', 'hidden')
The draws below stay inside these ranges and needn't reach their ends.
Inputs may be any that keep to these rules, and one draw needn't show every extreme that they name: `expert_ids`: in each aligned block of 128 tokens, every expert is named by no slot or by exactly 64 slots; a token's two experts differ; one expert is named by 64 slots in every block.
All inputs are finite; a program needn't handle non-finite values. No bound on the sum of `spike_mask` on one device may be relied on, other than what follows from the above.
Results may differ from the reference program's by a relative error of at most 0.015.
Values may be sent and summed in bfloat16 or wider, within the bound.
A program may use at most 128 MiB of HBM per device.

```python
import jax
import jax.numpy as jnp
from jax import lax

D = 4096
FF = 1024
TOP = 2
TOK_DEV = 128
EXPERTS = 8
TOKENS = 1024
CAP = 64
N_EXPERT = 8
N_HIDDEN = 4


def draw_expert_ids(key, part):
    key_hot, key_blocks = jax.random.split(jax.random.fold_in(key, 11))
    hot = jax.random.randint(key_hot, (), 0, EXPERTS).astype(jnp.int32)

    def one_block(block_key):
        key_perm, key_order = jax.random.split(block_key)
        perm = jax.random.permutation(key_perm, EXPERTS).astype(jnp.int32)
        first = perm[0]
        perm = jnp.where(perm == hot, first, perm)
        perm = perm.at[0].set(hot)
        listing = perm[jnp.arange(2 * TOK_DEV, dtype=jnp.int32) // CAP]
        order = jax.random.permutation(key_order, TOK_DEV).astype(jnp.int32)
        return jnp.stack([listing[order], listing[order + TOK_DEV]], axis=1)
    keys = jax.random.split(key_blocks, EXPERTS)
    blocks = jax.vmap(one_block)(keys)
    return blocks.reshape(TOKENS, TOP).astype(jnp.int32)


def plant(result, rng, least, high):
    place = [jax.random.randint(jax.random.fold_in(rng, axis), (), 0, length) for axis, length in enumerate(result.shape)]
    widest = result.shape.index(max(result.shape))
    beside = place[:widest] + [(place[widest] + 1) % result.shape[widest]] + place[widest + 1:]
    return result.at[tuple(place)].set(least).at[tuple(beside)].set(high)


def shard_levels(own_key, shape, cuts, low, largest):
    def one(dim, parts):
        draws = jax.random.uniform(jax.random.fold_in(jax.random.fold_in(own_key, 6), dim), (parts,), jnp.float32, low / len(cuts), largest / len(cuts))
        return jnp.repeat(jnp.exp(draws), shape[dim] // parts).reshape((-1,) + (1,) * (len(shape) - dim - 1))

    gain = one(*cuts[0])
    for cut in cuts[1:]:
        gain = gain * one(*cut)
    return gain


def centred(own_key, dims, spread, most, cuts=(), kind=jnp.bfloat16):
    entries = jax.random.normal(own_key, dims, jnp.float32) * spread
    if len(cuts) > 0:
        entries = shard_levels(own_key, dims, cuts, -0.22, 0.18) * entries
    return jnp.clip(entries, min=-most, max=most).astype(kind)


def setup_inputs(seed: int = 0) -> dict:
    key_of = jax.random.split(jax.random.key(seed), 9)
    tokens = centred(key_of[0], (TOKENS, D), 1.0, 6.0, ((0, 8),))
    cotangent = centred(key_of[1], (TOKENS, D), 0.5, 3.0, ((0, 8),))
    expert_ids = draw_expert_ids(jax.random.fold_in(key_of[8], 71), 0)
    gate_codes = plant(jax.random.randint(key_of[3], (TOKENS, TOP), 1, 257), jax.random.fold_in(key_of[3], 1), 1, 256).astype(jnp.int32)
    up_weight = centred(key_of[4], (EXPERTS, D, FF), D ** -0.5, 0.09375, ((0, 8), (2, 4)))
    down_weight = centred(key_of[5], (EXPERTS, FF, D), FF ** -0.5, 0.1875, ((0, 8), (1, 4)))
    threshold_state = plant(jax.random.randint(key_of[6], (EXPERTS, FF), -64, 192), jax.random.fold_in(key_of[6], 1), -64, 191).astype(jnp.int32)
    spike_mask = plant((jax.random.randint(key_of[7], (EXPERTS, FF), 0, 4) < 3).astype(jnp.int32), jax.random.fold_in(key_of[7], 1), 0, 1)
    return {"tokens": tokens, "cotangent": cotangent, "expert_ids": expert_ids, "gate_codes": gate_codes, "up_weight": up_weight, "down_weight": down_weight, "threshold_state": threshold_state, "spike_mask": spike_mask}


SHARPNESS = 2.0


def reference(tokens, cotangent, expert_ids, gate_codes, up_weight, down_weight, threshold_state, spike_mask):
    pairs = TOKENS * TOP
    most = N_EXPERT * CAP
    share = FF // N_HIDDEN
    flat_ids = expert_ids.reshape(pairs).astype(jnp.int32)
    pair_index = jnp.arange(pairs, dtype=jnp.int32)
    order = jnp.argsort(flat_ids * pairs + pair_index).astype(jnp.int32)
    counts = jnp.sum((flat_ids[None, :] == jnp.arange(EXPERTS, dtype=jnp.int32)[:, None]).astype(jnp.int32), axis=1)
    starts = (jnp.cumsum(counts) - counts).astype(jnp.int32)
    padded_order = jnp.concatenate([order, jnp.zeros((most,), jnp.int32)])
    gates = gate_codes.reshape(pairs).astype(jnp.float32) / 256.0

    def one_expert(carry, expert):
        out_total, in_total = carry
        picked = lax.dynamic_slice(padded_order, (starts[expert],), (most,))
        live = jnp.arange(most, dtype=jnp.int32) < counts[expert]
        rows = (picked // TOP).astype(jnp.int32)
        weight = jnp.where(live, gates[picked], 0.0)[:, None]
        inputs = jnp.where(live[:, None], tokens[rows], 0).astype(jnp.bfloat16)
        upstream = jnp.where(live[:, None], cotangent[rows], 0).astype(jnp.bfloat16)
        up_block = up_weight[expert]
        down_block = down_weight[expert]
        level = threshold_state[expert].astype(jnp.float32) / 64.0
        opened = spike_mask[expert].astype(jnp.float32)
        pre = jnp.dot(inputs, up_block, preferred_element_type=jnp.float32)
        sigma = jax.nn.sigmoid(SHARPNESS * (pre - level))
        gated = (weight * opened * pre * sigma).astype(jnp.bfloat16)
        back_hidden = jnp.dot(upstream, down_block.T, preferred_element_type=jnp.float32) * weight
        slope = opened * (sigma + SHARPNESS * pre * sigma * (1.0 - sigma))
        dpre = (back_hidden * slope).astype(jnp.bfloat16)
        out_rows = jnp.zeros((most, D), jnp.float32)
        in_rows = jnp.zeros((most, D), jnp.float32)
        for quarter in range(N_HIDDEN):
            low = quarter * share
            piece = jnp.dot(gated[:, low:low + share], down_block[low:low + share, :], preferred_element_type=jnp.float32).astype(jnp.bfloat16)
            out_rows = out_rows + lax.optimization_barrier(piece).astype(jnp.float32)
            piece = jnp.dot(dpre[:, low:low + share], up_block[:, low:low + share].T, preferred_element_type=jnp.float32).astype(jnp.bfloat16)
            in_rows = in_rows + lax.optimization_barrier(piece).astype(jnp.float32)
        out_total = out_total.at[rows].add(jnp.where(live[:, None], out_rows, 0.0))
        in_total = in_total.at[rows].add(jnp.where(live[:, None], in_rows, 0.0))
        grad_down = jnp.dot(gated.T, upstream, preferred_element_type=jnp.float32).astype(jnp.bfloat16)
        grad_up = jnp.dot(inputs.T, dpre, preferred_element_type=jnp.float32).astype(jnp.bfloat16)
        return (out_total, in_total), (grad_up, grad_down)

    zeros = jnp.zeros((TOKENS, D), jnp.float32)
    carry, grads = lax.scan(one_expert, (zeros, zeros), jnp.arange(EXPERTS, dtype=jnp.int32))
    out_total, in_total = carry
    grad_up, grad_down = grads
    return out_total.astype(jnp.bfloat16), in_total.astype(jnp.bfloat16), grad_up, grad_down
```

```python
import functools

import jax
import jax.numpy as jnp
from jax import lax
from jax.experimental import pallas as pl
from jax.experimental.pallas import tpu as pltpu
from jax.sharding import PartitionSpec as P

SHARPNESS = 2.0
LANES = 128
MESH = pl.DeviceIdType.MESH


def greet(groups, me, h, core_mate, far_mate):
    barrier = pltpu.get_barrier_semaphore()

    def hello(d, carry):
        peer = lax.rem(me + d, groups)
        pl.semaphore_signal(barrier, inc=1, device_id=(peer, h), device_id_type=MESH)
        return carry

    lax.fori_loop(1, groups, hello, 0)
    for mate in (core_mate, far_mate):
        pl.semaphore_signal(barrier, inc=1, device_id=(me, mate), device_id_type=MESH)
    pl.semaphore_wait(barrier, groups + 1)


def places():
    me = lax.axis_index("expert")
    h = lax.axis_index("hidden")
    core_mate = h + 1 - 2 * lax.rem(h, 2)
    far_mate = lax.rem(h + 2, 4)
    return me, h, core_mate, far_mate


def columns(index, width):
    return pl.ds(pl.multiple_of(index * width, width), width)


def dispatch_kernel(
    groups,
    send_in,
    send_up,
    send_gate,
    own_in,
    own_up,
    got_in,
    got_up,
    got_gate,
    far_send,
    far_recv,
    y_send,
    y_recv,
    c_send,
    c_recv,
    r_send,
    r_recv,
    own_sem,
):
    me, h, core_mate, far_mate = places()
    quarter = send_in.shape[2]
    greet(groups, me, h, core_mate, far_mate)
    mine = columns(h, quarter)
    theirs = columns(far_mate, quarter)
    tensors = ((send_in, got_in, own_in), (send_up, got_up, own_up))

    def out_copies(d):
        peer = lax.rem(me + d, groups)
        made = [
            pltpu.make_async_remote_copy(
                src_ref=src.at[peer],
                dst_ref=dst.at[me, :, mine],
                send_sem=far_send.at[t, d],
                recv_sem=far_recv.at[t, d],
                device_id=(peer, h),
                device_id_type=MESH,
            )
            for t, (src, dst, own) in enumerate(tensors)
        ]
        made.append(
            pltpu.make_async_remote_copy(
                src_ref=send_gate.at[peer],
                dst_ref=got_gate.at[me],
                send_sem=far_send.at[2, d],
                recv_sem=far_recv.at[2, d],
                device_id=(peer, h),
                device_id_type=MESH,
            )
        )
        return made

    def share(d, t, cols, mate, s_sem, r_sem):
        owner = lax.rem(me + groups - d, groups)
        block = tensors[t][1].at[owner, :, cols]
        return pltpu.make_async_remote_copy(
            src_ref=block,
            dst_ref=block,
            send_sem=s_sem.at[t, d],
            recv_sem=r_sem.at[t, d],
            device_id=(me, mate),
            device_id_type=MESH,
        )

    def begin(d, carry):
        for copy in out_copies(d):
            copy.start()
        return carry

    lax.fori_loop(1, groups, begin, 0)
    own_copies = [
        pltpu.make_async_copy(own_in, got_in.at[me], own_sem.at[0]),
        pltpu.make_async_copy(own_up, got_up.at[me], own_sem.at[1]),
        pltpu.make_async_copy(send_gate.at[me], got_gate.at[me], own_sem.at[2]),
    ]
    for copy in own_copies:
        copy.start()

    def relay(d):
        for t in range(2):
            share(d, t, mine, far_mate, y_send, y_recv).wait_recv()
            share(d, t, theirs, core_mate, r_send, r_recv).start()

    def forward(d, carry):
        arrived = out_copies(d)
        for t in range(2):
            arrived[t].wait_recv()
            share(d, t, mine, far_mate, y_send, y_recv).start()
            share(d, t, mine, core_mate, c_send, c_recv).start()

        @pl.when(d > 1)
        def _():
            relay(d - 1)

        return carry

    lax.fori_loop(1, groups, forward, 0)
    relay(groups - 1)

    def finish(d, carry):
        for copy in out_copies(d):
            copy.wait_send()
        out_copies(d)[2].wait_recv()
        for t in range(2):
            share(d, t, mine, far_mate, y_send, y_recv).wait_send()
            share(d, t, mine, core_mate, c_send, c_recv).wait()
            share(d, t, theirs, core_mate, r_send, r_recv).wait()
        return carry

    lax.fori_loop(1, groups, finish, 0)
    for copy in own_copies:
        copy.wait()


def dispatch(groups, send_in, send_up, send_gate, own_in, own_up):
    capacity, quarter = send_in.shape[1:]
    width = own_in.shape[1]
    anywhere = pl.BlockSpec(memory_space=pl.ANY)
    dma = pltpu.SemaphoreType.DMA
    return pl.pallas_call(
        functools.partial(dispatch_kernel, groups),
        out_shape=(
            jax.ShapeDtypeStruct((groups, capacity, width), jnp.bfloat16),
            jax.ShapeDtypeStruct((groups, capacity, width), jnp.bfloat16),
            jax.ShapeDtypeStruct((groups, capacity, LANES), jnp.bfloat16),
        ),
        in_specs=[anywhere] * 5,
        out_specs=(anywhere,) * 3,
        scratch_shapes=[dma((3, groups)), dma((3, groups))]
        + [dma((2, groups))] * 6
        + [dma((3,))],
        compiler_params=pltpu.CompilerParams(collective_id=0, has_side_effects=True),
    )(send_in, send_up, send_gate, own_in, own_up)


def combine_kernel(
    groups,
    part_out,
    part_back,
    home_out,
    home_back,
    core_in,
    far_out,
    far_in,
    total,
    c_send,
    c_recv,
    y_send,
    y_recv,
    far_send,
    far_recv,
):
    me, h, core_mate, far_mate = places()
    quarter = home_out.shape[2]
    parts = (part_out, part_back)
    homes = (home_out, home_back)
    greet(groups, me, h, core_mate, far_mate)
    far_core_mate = lax.rem(core_mate + 2, 4)
    mate_quarters = (core_mate, far_core_mate)

    def owner_of(d):
        return lax.rem(me + d, groups)

    def core_copy(d, t, which):
        owner = owner_of(d)
        return pltpu.make_async_remote_copy(
            src_ref=parts[t].at[owner, :, columns(mate_quarters[which], quarter)],
            dst_ref=core_in.at[t, which, owner],
            send_sem=c_send.at[t, which, d],
            recv_sem=c_recv.at[t, which, d],
            device_id=(me, core_mate),
            device_id_type=MESH,
        )

    def far_copy(d, t):
        owner = owner_of(d)
        return pltpu.make_async_remote_copy(
            src_ref=far_out.at[t, owner],
            dst_ref=far_in.at[t, owner],
            send_sem=y_send.at[t, d],
            recv_sem=y_recv.at[t, d],
            device_id=(me, far_mate),
            device_id_type=MESH,
        )

    def home_copy(d, t):
        owner = owner_of(d)
        return pltpu.make_async_remote_copy(
            src_ref=total.at[t, owner],
            dst_ref=homes[t].at[me],
            send_sem=far_send.at[t, d],
            recv_sem=far_recv.at[t, d],
            device_id=(owner, h),
            device_id_type=MESH,
        )

    def begin(i, carry):
        d = lax.rem(i + 1, groups)
        for t in range(2):
            for which in (1, 0):
                core_copy(d, t, which).start()
        return carry

    lax.fori_loop(0, groups, begin, 0)

    def first(i):
        d = lax.rem(i + 1, groups)
        owner = owner_of(d)
        for t in range(2):
            core_copy(d, t, 1).wait_recv()
            far_out[t, owner] = (
                parts[t][owner, :, columns(far_mate, quarter)].astype(jnp.float32)
                + core_in[t, 1, owner].astype(jnp.float32)
            ).astype(jnp.bfloat16)
            far_copy(d, t).start()

    def second(i, last):
        d = lax.rem(i + 1, groups)
        owner = owner_of(d)
        for t in range(2):
            core_copy(d, t, 0).wait_recv()
            far_copy(d, t).wait_recv()
            value = (
                parts[t][owner, :, columns(h, quarter)].astype(jnp.float32)
                + core_in[t, 0, owner].astype(jnp.float32)
                + far_in[t, owner].astype(jnp.float32)
            ).astype(jnp.bfloat16)
            if last:
                homes[t][owner] = value
            else:
                total[t, owner] = value
                home_copy(d, t).start()

    first(0)

    def step(i, carry):
        first(i + 1)
        second(i, False)
        return carry

    lax.fori_loop(0, groups - 1, step, 0)
    second(groups - 1, True)

    def finish(i, carry):
        d = lax.rem(i + 1, groups)
        for t in range(2):
            for which in (0, 1):
                core_copy(d, t, which).wait_send()
            far_copy(d, t).wait_send()
        return carry

    lax.fori_loop(0, groups, finish, 0)

    def close(d, carry):
        for t in range(2):
            home_copy(d, t).wait()
        return carry

    lax.fori_loop(1, groups, close, 0)


def combine(groups, part_out, part_back):
    capacity, width = part_out.shape[1:]
    quarter = width // 4
    vmem = pl.BlockSpec(memory_space=pltpu.VMEM)
    dma = pltpu.SemaphoreType.DMA
    block = (groups, capacity, quarter)
    return pl.pallas_call(
        functools.partial(combine_kernel, groups),
        out_shape=(jax.ShapeDtypeStruct(block, jnp.bfloat16),) * 2,
        in_specs=[vmem] * 2,
        out_specs=(vmem,) * 2,
        scratch_shapes=[
            pltpu.VMEM((2, 2) + block, jnp.bfloat16),
            pltpu.VMEM((2,) + block, jnp.bfloat16),
            pltpu.VMEM((2,) + block, jnp.bfloat16),
            pltpu.VMEM((2,) + block, jnp.bfloat16),
            dma((2, 2, groups)),
            dma((2, 2, groups)),
            dma((2, groups)),
            dma((2, groups)),
            dma((2, groups)),
            dma((2, groups)),
        ],
        compiler_params=pltpu.CompilerParams(
            collective_id=1, has_side_effects=True, vmem_limit_bytes=48 * 2**20
        ),
    )(part_out, part_back)


def expert_pass(inputs, upstream, weight_col, up_block, down_block, threshold_row, mask_row):
    pre = jnp.dot(inputs, up_block, preferred_element_type=jnp.float32)
    level = threshold_row.astype(jnp.float32) / 64.0
    opened = mask_row.astype(jnp.float32)
    sigma = jax.nn.sigmoid(SHARPNESS * (pre - level))
    gated = (weight_col * opened * pre * sigma).astype(jnp.bfloat16)
    back_hidden = (
        jnp.einsum("rd,fd->rf", upstream, down_block, preferred_element_type=jnp.float32)
        * weight_col
    )
    slope = opened * (sigma + SHARPNESS * pre * sigma * (1.0 - sigma))
    dpre = (back_hidden * slope).astype(jnp.bfloat16)
    part_out = jnp.dot(gated, down_block, preferred_element_type=jnp.float32)
    part_back = jnp.einsum("rf,df->rd", dpre, up_block, preferred_element_type=jnp.float32)
    grad_down = jnp.einsum("rf,rd->fd", gated, upstream, preferred_element_type=jnp.float32).astype(
        jnp.bfloat16
    )
    grad_up = jnp.einsum("rd,rf->df", inputs, dpre, preferred_element_type=jnp.float32).astype(
        jnp.bfloat16
    )
    return (part_out, part_back, grad_up, grad_down)


def shards(
    tokens, cotangent, expert_ids, gate_codes, up_weight, down_weight, threshold_state, spike_mask
):
    groups = lax.axis_size("expert")
    me = lax.axis_index("expert")
    h = lax.axis_index("hidden")
    tok_rows, width = tokens.shape
    quarter = width // lax.axis_size("hidden")
    top = expert_ids.shape[1]
    capacity = 4 * tok_rows // groups
    pairs = tok_rows * top
    slots = groups * capacity
    flat_ids = expert_ids.reshape(pairs)
    pair_index = jnp.arange(pairs, dtype=jnp.int32)
    earlier = (flat_ids[None, :] == flat_ids[:, None]) & (pair_index[None, :] < pair_index[:, None])
    place = jnp.sum(earlier.astype(jnp.int32), axis=1)
    target = (flat_ids * capacity + place).reshape(tok_rows, top)
    slot_index = jnp.arange(slots, dtype=jnp.int32)
    gates = gate_codes.astype(jnp.float32) / 256.0
    hits = [target[None, :, k] == slot_index[:, None] for k in range(top)]
    pick = functools.reduce(jnp.logical_or, hits).astype(jnp.bfloat16)
    slot_gate = sum(
        jnp.sum(jnp.where(hits[k], gates[None, :, k], 0.0), axis=1) for k in range(top)
    ).astype(jnp.bfloat16)
    send_gate = jnp.broadcast_to(slot_gate[:, None], (slots, LANES)).reshape(
        groups, capacity, LANES
    )

    def choose(which, rows):
        return jnp.dot(which, rows, preferred_element_type=jnp.float32).astype(jnp.bfloat16)

    own_pick = lax.dynamic_slice_in_dim(pick, me * capacity, capacity, 0)
    tok_cut = lax.dynamic_slice_in_dim(tokens, h * quarter, quarter, 1)
    cot_cut = lax.dynamic_slice_in_dim(cotangent, h * quarter, quarter, 1)
    got_in, got_up, got_gate = dispatch(
        groups,
        choose(pick, tok_cut).reshape(groups, capacity, quarter),
        choose(pick, cot_cut).reshape(groups, capacity, quarter),
        send_gate,
        choose(own_pick, tokens),
        choose(own_pick, cotangent),
    )
    part_out, part_back, grad_up, grad_down = expert_pass(
        got_in.reshape(slots, width),
        got_up.reshape(slots, width),
        got_gate.reshape(slots, LANES)[:, :1].astype(jnp.float32),
        up_weight[0],
        down_weight[0],
        threshold_state[0],
        spike_mask[0],
    )
    home_out, home_back = combine(
        groups,
        part_out.astype(jnp.bfloat16).reshape(groups, capacity, width),
        part_back.astype(jnp.bfloat16).reshape(groups, capacity, width),
    )

    def gather_home(home):
        return jnp.einsum(
            "st,sw->tw", pick, home.reshape(slots, quarter), preferred_element_type=jnp.float32
        ).astype(jnp.bfloat16)

    return (gather_home(home_out), gather_home(home_back), grad_up[None], grad_down[None])


def solution(mesh):
    placed = (
        P("expert", None),
        P("expert", None),
        P("expert", None),
        P("expert", None),
        P("expert", None, "hidden"),
        P("expert", "hidden", None),
        P("expert", "hidden"),
        P("expert", "hidden"),
    )
    return jax.shard_map(
        shards,
        mesh=mesh,
        in_specs=placed,
        out_specs=(
            P("expert", "hidden"),
            P("expert", "hidden"),
            P("expert", None, "hidden"),
            P("expert", "hidden", None),
        ),
        check_vma=False,
    )
```

```python
import functools

import jax
import jax.numpy as jnp
from jax import lax
from jax.experimental import pallas as pl
from jax.experimental.pallas import tpu as pltpu
from jax.sharding import PartitionSpec as P

SHARPNESS = 2.0
LANES = 128
MESH = pl.DeviceIdType.MESH


def greet(groups, me, h, core_mate, far_mate):
    barrier = pltpu.get_barrier_semaphore()

    def hello(d, carry):
        peer = lax.rem(me + d, groups)
        pl.semaphore_signal(barrier, inc=1, device_id=(peer, h), device_id_type=MESH)
        return carry

    lax.fori_loop(1, groups, hello, 0)
    for mate in (core_mate, far_mate):
        pl.semaphore_signal(barrier, inc=1, device_id=(me, mate), device_id_type=MESH)
    pl.semaphore_wait(barrier, groups + 1)


def places():
    me = lax.axis_index("expert")
    h = lax.axis_index("hidden")
    core_mate = h + 1 - 2 * lax.rem(h, 2)
    far_mate = lax.rem(h + 2, 4)
    return me, h, core_mate, far_mate


def columns(index, width):
    return pl.ds(pl.multiple_of(index * width, width), width)


def dispatch_kernel(
    groups,
    send_in,
    send_up,
    send_gate,
    own_in,
    own_up,
    got_in,
    got_up,
    got_gate,
    far_send,
    far_recv,
    y_send,
    y_recv,
    c_send,
    c_recv,
    r_send,
    r_recv,
    own_sem,
):
    me, h, core_mate, far_mate = places()
    quarter = send_in.shape[2]
    greet(groups, me, h, core_mate, far_mate)
    mine = columns(h, quarter)
    theirs = columns(far_mate, quarter)
    tensors = ((send_in, got_in, own_in), (send_up, got_up, own_up))

    def out_copies(d):
        peer = lax.rem(me + d, groups)
        made = [
            pltpu.make_async_remote_copy(
                src_ref=src.at[peer],
                dst_ref=dst.at[me, :, mine],
                send_sem=far_send.at[t, d],
                recv_sem=far_recv.at[t, d],
                device_id=(peer, h),
                device_id_type=MESH,
            )
            for t, (src, dst, own) in enumerate(tensors)
        ]
        made.append(
            pltpu.make_async_remote_copy(
                src_ref=send_gate.at[peer],
                dst_ref=got_gate.at[me],
                send_sem=far_send.at[2, d],
                recv_sem=far_recv.at[2, d],
                device_id=(peer, h),
                device_id_type=MESH,
            )
        )
        return made

    def share(d, t, cols, mate, s_sem, r_sem):
        owner = lax.rem(me + groups - d, groups)
        block = tensors[t][1].at[owner, :, cols]
        return pltpu.make_async_remote_copy(
            src_ref=block,
            dst_ref=block,
            send_sem=s_sem.at[t, d],
            recv_sem=r_sem.at[t, d],
            device_id=(me, mate),
            device_id_type=MESH,
        )

    def begin(d, carry):
        for copy in out_copies(d):
            copy.start()
        return carry

    lax.fori_loop(1, groups, begin, 0)
    own_copies = [
        pltpu.make_async_copy(own_in, got_in.at[me], own_sem.at[0]),
        pltpu.make_async_copy(own_up, got_up.at[me], own_sem.at[1]),
        pltpu.make_async_copy(send_gate.at[me], got_gate.at[me], own_sem.at[2]),
    ]
    for copy in own_copies:
        copy.start()

    def relay(d):
        for t in range(2):
            share(d, t, mine, far_mate, y_send, y_recv).wait_recv()
            share(d, t, theirs, core_mate, r_send, r_recv).start()

    def forward(d, carry):
        arrived = out_copies(d)
        for t in range(2):
            arrived[t].wait_recv()
            share(d, t, mine, far_mate, y_send, y_recv).start()
            share(d, t, mine, core_mate, c_send, c_recv).start()

        @pl.when(d > 1)
        def _():
            relay(d - 1)

        return carry

    lax.fori_loop(1, groups, forward, 0)
    relay(groups - 1)

    def finish(d, carry):
        for copy in out_copies(d):
            copy.wait_send()
        out_copies(d)[2].wait_recv()
        for t in range(2):
            share(d, t, mine, far_mate, y_send, y_recv).wait_send()
            share(d, t, mine, core_mate, c_send, c_recv).wait()
            share(d, t, theirs, core_mate, r_send, r_recv).wait()
        return carry

    lax.fori_loop(1, groups, finish, 0)
    for copy in own_copies:
        copy.wait()


def dispatch(groups, send_in, send_up, send_gate, own_in, own_up):
    capacity, quarter = send_in.shape[1:]
    width = own_in.shape[1]
    anywhere = pl.BlockSpec(memory_space=pl.ANY)
    dma = pltpu.SemaphoreType.DMA
    return pl.pallas_call(
        functools.partial(dispatch_kernel, groups),
        out_shape=(
            jax.ShapeDtypeStruct((groups, capacity, width), jnp.bfloat16),
            jax.ShapeDtypeStruct((groups, capacity, width), jnp.bfloat16),
            jax.ShapeDtypeStruct((groups, capacity, LANES), jnp.bfloat16),
        ),
        in_specs=[anywhere] * 5,
        out_specs=(anywhere,) * 3,
        scratch_shapes=[dma((3, groups)), dma((3, groups))]
        + [dma((2, groups))] * 6
        + [dma((3,))],
        compiler_params=pltpu.CompilerParams(collective_id=0, has_side_effects=True),
    )(send_in, send_up, send_gate, own_in, own_up)


def combine_kernel(
    groups,
    part_out,
    part_back,
    home_out,
    home_back,
    core_in,
    far_out,
    far_in,
    total,
    c_send,
    c_recv,
    y_send,
    y_recv,
    far_send,
    far_recv,
):
    me, h, core_mate, far_mate = places()
    quarter = home_out.shape[2]
    parts = (part_out, part_back)
    homes = (home_out, home_back)
    greet(groups, me, h, core_mate, far_mate)
    far_core_mate = lax.rem(core_mate + 2, 4)
    mate_quarters = (core_mate, far_core_mate)

    def owner_of(d):
        return lax.rem(me + d, groups)

    def core_copy(d, t, which):
        owner = owner_of(d)
        return pltpu.make_async_remote_copy(
            src_ref=parts[t].at[owner, :, columns(mate_quarters[which], quarter)],
            dst_ref=core_in.at[t, which, owner],
            send_sem=c_send.at[t, which, d],
            recv_sem=c_recv.at[t, which, d],
            device_id=(me, core_mate),
            device_id_type=MESH,
        )

    def far_copy(d, t):
        owner = owner_of(d)
        return pltpu.make_async_remote_copy(
            src_ref=far_out.at[t, owner],
            dst_ref=far_in.at[t, owner],
            send_sem=y_send.at[t, d],
            recv_sem=y_recv.at[t, d],
            device_id=(me, far_mate),
            device_id_type=MESH,
        )

    def home_copy(d, t):
        owner = owner_of(d)
        return pltpu.make_async_remote_copy(
            src_ref=total.at[t, owner],
            dst_ref=homes[t].at[me],
            send_sem=far_send.at[t, d],
            recv_sem=far_recv.at[t, d],
            device_id=(owner, h),
            device_id_type=MESH,
        )

    def begin(i, carry):
        d = lax.rem(i + 1, groups)
        for t in range(2):
            for which in (1, 0):
                core_copy(d, t, which).start()
        return carry

    lax.fori_loop(0, groups, begin, 0)

    def first(i):
        d = lax.rem(i + 1, groups)
        owner = owner_of(d)
        for t in range(2):
            core_copy(d, t, 1).wait_recv()
            far_out[t, owner] = (
                parts[t][owner, :, columns(far_mate, quarter)].astype(jnp.float32)
                + core_in[t, 1, owner].astype(jnp.float32)
            ).astype(jnp.bfloat16)
            far_copy(d, t).start()

    def second(i, last):
        d = lax.rem(i + 1, groups)
        owner = owner_of(d)
        for t in range(2):
            core_copy(d, t, 0).wait_recv()
            far_copy(d, t).wait_recv()
            value = (
                parts[t][owner, :, columns(h, quarter)].astype(jnp.float32)
                + core_in[t, 0, owner].astype(jnp.float32)
                + far_in[t, owner].astype(jnp.float32)
            ).astype(jnp.bfloat16)
            if last:
                homes[t][owner] = value
            else:
                total[t, owner] = value
                home_copy(d, t).start()

    first(0)

    def step(i, carry):
        first(i + 1)
        second(i, False)
        return carry

    lax.fori_loop(0, groups - 1, step, 0)
    second(groups - 1, True)

    def finish(i, carry):
        d = lax.rem(i + 1, groups)
        for t in range(2):
            for which in (0, 1):
                core_copy(d, t, which).wait_send()
            far_copy(d, t).wait_send()
        return carry

    lax.fori_loop(0, groups, finish, 0)

    def close(d, carry):
        for t in range(2):
            home_copy(d, t).wait()
        return carry

    lax.fori_loop(1, groups, close, 0)


def combine(groups, part_out, part_back):
    capacity, width = part_out.shape[1:]
    quarter = width // 4
    vmem = pl.BlockSpec(memory_space=pltpu.VMEM)
    dma = pltpu.SemaphoreType.DMA
    block = (groups, capacity, quarter)
    return pl.pallas_call(
        functools.partial(combine_kernel, groups),
        out_shape=(jax.ShapeDtypeStruct(block, jnp.bfloat16),) * 2,
        in_specs=[vmem] * 2,
        out_specs=(vmem,) * 2,
        scratch_shapes=[
            pltpu.VMEM((2, 2) + block, jnp.bfloat16),
            pltpu.VMEM((2,) + block, jnp.bfloat16),
            pltpu.VMEM((2,) + block, jnp.bfloat16),
            pltpu.VMEM((2,) + block, jnp.bfloat16),
            dma((2, 2, groups)),
            dma((2, 2, groups)),
            dma((2, groups)),
            dma((2, groups)),
            dma((2, groups)),
            dma((2, groups)),
        ],
        compiler_params=pltpu.CompilerParams(
            collective_id=1, has_side_effects=True, vmem_limit_bytes=48 * 2**20
        ),
    )(part_out, part_back)


def fused_kernel(
    groups,
    tokens,
    cotangent,
    pick,
    send_gate,
    level,
    opened,
    up_any,
    down_any,
    home_out,
    home_back,
    grad_up_t,
    grad_down,
    got_in,
    got_up,
    got_gate,
    send_buf,
    up,
    down,
    gated_all,
    dpre_all,
    part,
    core_in,
    far_out,
    far_in,
    total,
    w_sem,
    far_send,
    far_recv,
    y_send,
    y_recv,
    c_send,
    c_recv,
    r_send,
    r_recv,
    back_c_send,
    back_c_recv,
    back_y_send,
    back_y_recv,
    home_send,
    home_recv,
):
    me, h, core_mate, far_mate = places()
    quarter = home_out.shape[2]
    capacity = home_out.shape[1]
    width = tokens.shape[1]
    hidden_units = down.shape[0]
    slots = groups * capacity
    far_core_mate = lax.rem(core_mate + 2, 4)
    mate_quarters = (core_mate, far_core_mate)
    weight_copies = [
        pltpu.make_async_copy(up_any, up, w_sem.at[0]),
        pltpu.make_async_copy(down_any, down, w_sem.at[1]),
    ]
    for copy in weight_copies:
        copy.start()
    greet(groups, me, h, core_mate, far_mate)
    mine = columns(h, quarter)
    theirs = columns(far_mate, quarter)
    sources = (tokens, cotangent)
    gots = (got_in, got_up)
    homes = (home_out, home_back)

    def remote(src, dst, s_sem, r_sem, device):
        return pltpu.make_async_remote_copy(
            src_ref=src,
            dst_ref=dst,
            send_sem=s_sem,
            recv_sem=r_sem,
            device_id=device,
            device_id_type=MESH,
        )

    def owner_of(d):
        return lax.rem(me + groups - d, groups)

    def out_copy(d, t):
        peer = lax.rem(me + d, groups)
        if t == 2:
            src, dst = send_gate.at[peer], got_gate.at[me]
        else:
            src, dst = send_buf.at[t, peer], gots[t].at[me, :, mine]
        return remote(src, dst, far_send.at[t, d], far_recv.at[t, d], (peer, h))

    def share(d, t, cols, mate, s_sem, r_sem):
        block = gots[t].at[owner_of(d), :, cols]
        return remote(block, block, s_sem.at[t, d], r_sem.at[t, d], (me, mate))

    def y_share(d, t):
        return share(d, t, mine, far_mate, y_send, y_recv)

    def core_share(d, t):
        return share(d, t, mine, core_mate, c_send, c_recv)

    def relay_share(d, t):
        return share(d, t, theirs, core_mate, r_send, r_recv)

    def core_copy(d, t, which):
        owner = owner_of(d)
        return remote(
            part.at[t, owner, :, columns(mate_quarters[which], quarter)],
            core_in.at[t, which, owner],
            back_c_send.at[t, which, d],
            back_c_recv.at[t, which, d],
            (me, core_mate),
        )

    def far_copy(d, t):
        owner = owner_of(d)
        return remote(
            far_out.at[t, owner],
            far_in.at[t, owner],
            back_y_send.at[t, d],
            back_y_recv.at[t, d],
            (me, far_mate),
        )

    def home_copy(d, t):
        owner = owner_of(d)
        return remote(
            total.at[t, owner],
            homes[t].at[me],
            home_send.at[t, d],
            home_recv.at[t, d],
            (owner, h),
        )

    def times(a, b):
        return jnp.dot(a, b, preferred_element_type=jnp.float32)

    def times_t(a, b):
        return lax.dot_general(a, b, (((1,), (1,)), ((), ())), preferred_element_type=jnp.float32)

    def t_times(a, b):
        return lax.dot_general(a, b, (((0,), (0,)), ((), ())), preferred_element_type=jnp.float32)

    def begin(d, carry):
        peer = lax.rem(me + d, groups)
        for t in range(2):
            send_buf[t, peer] = times(pick[peer], sources[t][:, mine]).astype(jnp.bfloat16)
            out_copy(d, t).start()
        out_copy(d, 2).start()
        return carry

    lax.fori_loop(1, groups, begin, 0)
    for t in range(2):
        for q in range(4):
            cols = slice(q * quarter, (q + 1) * quarter)
            gots[t][me, :, cols] = times(pick[me], sources[t][:, cols]).astype(jnp.bfloat16)
    got_gate[me] = send_gate[me]
    for copy in weight_copies:
        copy.wait()

    def forward(d):
        for t in range(2):
            out_copy(d, t).wait_recv()
            y_share(d, t).start()
            core_share(d, t).start()

    def relay(d):
        for t in range(2):
            y_share(d, t).wait_recv()
            relay_share(d, t).start()

    def compute(d):
        owner = owner_of(d)
        weight_col = got_gate[owner].astype(jnp.float32)[:, :1]
        pre = times(got_in[owner], up[...])
        sigma = jax.nn.sigmoid(SHARPNESS * (pre - level[...]))
        gated = (weight_col * opened[...] * pre * sigma).astype(jnp.bfloat16)
        back_hidden = times_t(got_up[owner], down[...]) * weight_col
        slope = opened[...] * (sigma + SHARPNESS * pre * sigma * (1.0 - sigma))
        dpre = (back_hidden * slope).astype(jnp.bfloat16)
        gated_all[owner] = gated
        dpre_all[owner] = dpre
        for q in range(4):
            cols = slice(q * quarter, (q + 1) * quarter)
            part[0, owner, :, cols] = times(gated, down[:, cols]).astype(jnp.bfloat16)
            part[1, owner, :, cols] = times_t(dpre, up[cols, :]).astype(jnp.bfloat16)
        for t in range(2):
            for which in (1, 0):
                core_copy(d, t, which).start()

    def compute_arrived(d):
        for t in range(2):
            core_share(d, t).wait_recv()
            relay_share(d, t).wait_recv()
        out_copy(d, 2).wait_recv()
        compute(d)

    def first(d):
        owner = owner_of(d)
        for t in range(2):
            core_copy(d, t, 1).wait_recv()
            far_out[t, owner] = (
                part[t, owner, :, theirs].astype(jnp.float32)
                + core_in[t, 1, owner].astype(jnp.float32)
            ).astype(jnp.bfloat16)
            far_copy(d, t).start()

    def second(d):
        owner = owner_of(d)
        for t in range(2):
            core_copy(d, t, 0).wait_recv()
            far_copy(d, t).wait_recv()
            total[t, owner] = (
                part[t, owner, :, mine].astype(jnp.float32)
                + core_in[t, 0, owner].astype(jnp.float32)
                + far_in[t, owner].astype(jnp.float32)
            ).astype(jnp.bfloat16)

            @pl.when(d > 0)
            def _():
                home_copy(d, t).start()

    compute(0)

    def step(i, carry):
        pl.when(i < groups)(lambda: forward(i))
        pl.when((i > 1) & (i <= groups))(lambda: relay(i - 1))
        pl.when((i > 2) & (i <= groups + 1))(lambda: compute_arrived(i - 2))
        pl.when(i > 2)(lambda: first(i - 3))
        pl.when(i > 3)(lambda: second(i - 4))
        return carry

    lax.fori_loop(1, groups + 3, step, 0)
    tile = 512

    def grads(left, right, result):
        def one(n, carry):
            cols = columns(n, tile)
            rows = right[:, :, cols].reshape(slots, tile)
            result[:, cols] = t_times(left[...].reshape(slots, hidden_units), rows).astype(
                jnp.bfloat16
            )
            return carry

        lax.fori_loop(0, width // tile, one, 0)

    grads(gated_all, got_up, grad_down)
    second(groups - 1)
    grads(dpre_all, got_in, grad_up_t)
    for t in range(2):
        homes[t][me] = total[t, me]

    def finish(d, carry):
        for t in range(2):
            for which in (0, 1):
                core_copy(d, t, which).wait_send()
            far_copy(d, t).wait_send()

        @pl.when(d > 0)
        def _():
            for t in range(2):
                y_share(d, t).wait_send()
                core_share(d, t).wait_send()
                relay_share(d, t).wait_send()
                home_copy(d, t).wait()
            for t in range(3):
                out_copy(d, t).wait_send()

        return carry

    lax.fori_loop(0, groups, finish, 0)


def fused(groups, tokens, cotangent, pick, send_gate, level, opened, up_block, down_block):
    capacity = pick.shape[1]
    width = tokens.shape[1]
    quarter = width // 4
    hidden_units = down_block.shape[0]
    vmem = pl.BlockSpec(memory_space=pltpu.VMEM)
    anywhere = pl.BlockSpec(memory_space=pl.ANY)
    dma = pltpu.SemaphoreType.DMA
    block = (groups, capacity, quarter)
    whole = (groups, capacity, width)
    narrow = (groups, capacity, hidden_units)
    half = jnp.bfloat16
    return pl.pallas_call(
        functools.partial(fused_kernel, groups),
        out_shape=(
            jax.ShapeDtypeStruct(block, half),
            jax.ShapeDtypeStruct(block, half),
            jax.ShapeDtypeStruct((hidden_units, width), half),
            jax.ShapeDtypeStruct((hidden_units, width), half),
        ),
        in_specs=[vmem] * 6 + [anywhere] * 2,
        out_specs=(vmem,) * 4,
        scratch_shapes=[
            pltpu.VMEM(whole, half),
            pltpu.VMEM(whole, half),
            pltpu.VMEM((groups, capacity, LANES), half),
            pltpu.VMEM((2,) + block, half),
            pltpu.VMEM((width, hidden_units), half),
            pltpu.VMEM((hidden_units, width), half),
            pltpu.VMEM(narrow, half),
            pltpu.VMEM(narrow, half),
            pltpu.VMEM((2,) + whole, half),
            pltpu.VMEM((2, 2) + block, half),
            pltpu.VMEM((2,) + block, half),
            pltpu.VMEM((2,) + block, half),
            pltpu.VMEM((2,) + block, half),
            dma((2,)),
            dma((3, groups)),
            dma((3, groups)),
        ]
        + [dma((2, groups))] * 6
        + [dma((2, 2, groups))] * 2
        + [dma((2, groups))] * 4,
        compiler_params=pltpu.CompilerParams(
            collective_id=2, has_side_effects=True, vmem_limit_bytes=58 * 2**20
        ),
    )(tokens, cotangent, pick, send_gate, level, opened, up_block, down_block)


def expert_pass(inputs, upstream, weight_col, up_block, down_block, threshold_row, mask_row):
    pre = jnp.dot(inputs, up_block, preferred_element_type=jnp.float32)
    level = threshold_row.astype(jnp.float32) / 64.0
    opened = mask_row.astype(jnp.float32)
    sigma = jax.nn.sigmoid(SHARPNESS * (pre - level))
    gated = (weight_col * opened * pre * sigma).astype(jnp.bfloat16)
    back_hidden = (
        jnp.einsum("rd,fd->rf", upstream, down_block, preferred_element_type=jnp.float32)
        * weight_col
    )
    slope = opened * (sigma + SHARPNESS * pre * sigma * (1.0 - sigma))
    dpre = (back_hidden * slope).astype(jnp.bfloat16)
    part_out = jnp.dot(gated, down_block, preferred_element_type=jnp.float32)
    part_back = jnp.einsum("rf,df->rd", dpre, up_block, preferred_element_type=jnp.float32)
    grad_down = jnp.einsum("rf,rd->fd", gated, upstream, preferred_element_type=jnp.float32).astype(
        jnp.bfloat16
    )
    grad_up = jnp.einsum("rd,rf->df", inputs, dpre, preferred_element_type=jnp.float32).astype(
        jnp.bfloat16
    )
    return (part_out, part_back, grad_up, grad_down)


def shards(
    tokens, cotangent, expert_ids, gate_codes, up_weight, down_weight, threshold_state, spike_mask
):
    groups = lax.axis_size("expert")
    me = lax.axis_index("expert")
    h = lax.axis_index("hidden")
    tok_rows, width = tokens.shape
    quarter = width // lax.axis_size("hidden")
    top = expert_ids.shape[1]
    capacity = 4 * tok_rows // groups
    pairs = tok_rows * top
    slots = groups * capacity
    flat_ids = expert_ids.reshape(pairs)
    pair_index = jnp.arange(pairs, dtype=jnp.int32)
    earlier = (flat_ids[None, :] == flat_ids[:, None]) & (pair_index[None, :] < pair_index[:, None])
    place = jnp.sum(earlier.astype(jnp.int32), axis=1)
    target = (flat_ids * capacity + place).reshape(tok_rows, top)
    slot_index = jnp.arange(slots, dtype=jnp.int32)
    gates = gate_codes.astype(jnp.float32) / 256.0
    hits = [target[None, :, k] == slot_index[:, None] for k in range(top)]
    pick = functools.reduce(jnp.logical_or, hits).astype(jnp.bfloat16)
    slot_gate = sum(
        jnp.sum(jnp.where(hits[k], gates[None, :, k], 0.0), axis=1) for k in range(top)
    ).astype(jnp.bfloat16)
    send_gate = jnp.broadcast_to(slot_gate[:, None], (slots, LANES)).reshape(
        groups, capacity, LANES
    )

    def choose(which, rows):
        return jnp.dot(which, rows, preferred_element_type=jnp.float32).astype(jnp.bfloat16)

    if capacity % 16 == 0:
        home_out, home_back, grad_up_t, grad_down = fused(
            groups,
            tokens,
            cotangent,
            pick.reshape(groups, capacity, tok_rows),
            send_gate,
            threshold_state.astype(jnp.float32) / 64.0,
            spike_mask.astype(jnp.float32),
            up_weight[0],
            down_weight[0],
        )
        grad_up = grad_up_t.T
    else:
        own_pick = lax.dynamic_slice_in_dim(pick, me * capacity, capacity, 0)
        tok_cut = lax.dynamic_slice_in_dim(tokens, h * quarter, quarter, 1)
        cot_cut = lax.dynamic_slice_in_dim(cotangent, h * quarter, quarter, 1)
        got_in, got_up, got_gate = dispatch(
            groups,
            choose(pick, tok_cut).reshape(groups, capacity, quarter),
            choose(pick, cot_cut).reshape(groups, capacity, quarter),
            send_gate,
            choose(own_pick, tokens),
            choose(own_pick, cotangent),
        )
        part_out, part_back, grad_up, grad_down = expert_pass(
            got_in.reshape(slots, width),
            got_up.reshape(slots, width),
            got_gate.reshape(slots, LANES)[:, :1].astype(jnp.float32),
            up_weight[0],
            down_weight[0],
            threshold_state[0],
            spike_mask[0],
        )
        home_out, home_back = combine(
            groups,
            part_out.astype(jnp.bfloat16).reshape(groups, capacity, width),
            part_back.astype(jnp.bfloat16).reshape(groups, capacity, width),
        )

    def gather_home(home):
        return jnp.einsum(
            "st,sw->tw", pick, home.reshape(slots, quarter), preferred_element_type=jnp.float32
        ).astype(jnp.bfloat16)

    return (gather_home(home_out), gather_home(home_back), grad_up[None], grad_down[None])


def solution(mesh):
    placed = (
        P("expert", None),
        P("expert", None),
        P("expert", None),
        P("expert", None),
        P("expert", None, "hidden"),
        P("expert", "hidden", None),
        P("expert", "hidden"),
        P("expert", "hidden"),
    )
    return jax.shard_map(
        shards,
        mesh=mesh,
        in_specs=placed,
        out_specs=(
            P("expert", "hidden"),
            P("expert", "hidden"),
            P("expert", None, "hidden"),
            P("expert", "hidden", None),
        ),
        check_vma=False,
    )
```

```python
import functools

import jax
import jax.numpy as jnp
from jax import lax
from jax.experimental import pallas as pl
from jax.experimental.pallas import tpu as pltpu
from jax.sharding import PartitionSpec as P

SHARPNESS = 2.0
LANES = 128
MESH = pl.DeviceIdType.MESH


def greet(groups, me, h, core_mate, far_mate):
    barrier = pltpu.get_barrier_semaphore()

    def hello(d, carry):
        peer = lax.rem(me + d, groups)
        pl.semaphore_signal(barrier, inc=1, device_id=(peer, h), device_id_type=MESH)
        return carry

    lax.fori_loop(1, groups, hello, 0)
    for mate in (core_mate, far_mate):
        pl.semaphore_signal(barrier, inc=1, device_id=(me, mate), device_id_type=MESH)
    pl.semaphore_wait(barrier, groups + 1)


def places():
    me = lax.axis_index("expert")
    h = lax.axis_index("hidden")
    core_mate = h + 1 - 2 * lax.rem(h, 2)
    far_mate = lax.rem(h + 2, 4)
    return me, h, core_mate, far_mate


def columns(index, width):
    return pl.ds(pl.multiple_of(index * width, width), width)


def dispatch_kernel(
    groups,
    send_in,
    send_up,
    send_gate,
    own_in,
    own_up,
    got_in,
    got_up,
    got_gate,
    far_send,
    far_recv,
    y_send,
    y_recv,
    c_send,
    c_recv,
    r_send,
    r_recv,
    own_sem,
):
    me, h, core_mate, far_mate = places()
    quarter = send_in.shape[2]
    greet(groups, me, h, core_mate, far_mate)
    mine = columns(h, quarter)
    theirs = columns(far_mate, quarter)
    tensors = ((send_in, got_in, own_in), (send_up, got_up, own_up))

    def out_copies(d):
        peer = lax.rem(me + d, groups)
        made = [
            pltpu.make_async_remote_copy(
                src_ref=src.at[peer],
                dst_ref=dst.at[me, :, mine],
                send_sem=far_send.at[t, d],
                recv_sem=far_recv.at[t, d],
                device_id=(peer, h),
                device_id_type=MESH,
            )
            for t, (src, dst, own) in enumerate(tensors)
        ]
        made.append(
            pltpu.make_async_remote_copy(
                src_ref=send_gate.at[peer],
                dst_ref=got_gate.at[me],
                send_sem=far_send.at[2, d],
                recv_sem=far_recv.at[2, d],
                device_id=(peer, h),
                device_id_type=MESH,
            )
        )
        return made

    def share(d, t, cols, mate, s_sem, r_sem):
        owner = lax.rem(me + groups - d, groups)
        block = tensors[t][1].at[owner, :, cols]
        return pltpu.make_async_remote_copy(
            src_ref=block,
            dst_ref=block,
            send_sem=s_sem.at[t, d],
            recv_sem=r_sem.at[t, d],
            device_id=(me, mate),
            device_id_type=MESH,
        )

    def begin(d, carry):
        for copy in out_copies(d):
            copy.start()
        return carry

    lax.fori_loop(1, groups, begin, 0)
    own_copies = [
        pltpu.make_async_copy(own_in, got_in.at[me], own_sem.at[0]),
        pltpu.make_async_copy(own_up, got_up.at[me], own_sem.at[1]),
        pltpu.make_async_copy(send_gate.at[me], got_gate.at[me], own_sem.at[2]),
    ]
    for copy in own_copies:
        copy.start()

    def relay(d):
        for t in range(2):
            share(d, t, mine, far_mate, y_send, y_recv).wait_recv()
            share(d, t, theirs, core_mate, r_send, r_recv).start()

    def forward(d, carry):
        arrived = out_copies(d)
        for t in range(2):
            arrived[t].wait_recv()
            share(d, t, mine, far_mate, y_send, y_recv).start()
            share(d, t, mine, core_mate, c_send, c_recv).start()

        @pl.when(d > 1)
        def _():
            relay(d - 1)

        return carry

    lax.fori_loop(1, groups, forward, 0)
    relay(groups - 1)

    def finish(d, carry):
        for copy in out_copies(d):
            copy.wait_send()
        out_copies(d)[2].wait_recv()
        for t in range(2):
            share(d, t, mine, far_mate, y_send, y_recv).wait_send()
            share(d, t, mine, core_mate, c_send, c_recv).wait()
            share(d, t, theirs, core_mate, r_send, r_recv).wait()
        return carry

    lax.fori_loop(1, groups, finish, 0)
    for copy in own_copies:
        copy.wait()


def dispatch(groups, send_in, send_up, send_gate, own_in, own_up):
    capacity, quarter = send_in.shape[1:]
    width = own_in.shape[1]
    anywhere = pl.BlockSpec(memory_space=pl.ANY)
    dma = pltpu.SemaphoreType.DMA
    return pl.pallas_call(
        functools.partial(dispatch_kernel, groups),
        out_shape=(
            jax.ShapeDtypeStruct((groups, capacity, width), jnp.bfloat16),
            jax.ShapeDtypeStruct((groups, capacity, width), jnp.bfloat16),
            jax.ShapeDtypeStruct((groups, capacity, LANES), jnp.bfloat16),
        ),
        in_specs=[anywhere] * 5,
        out_specs=(anywhere,) * 3,
        scratch_shapes=[dma((3, groups)), dma((3, groups))]
        + [dma((2, groups))] * 6
        + [dma((3,))],
        compiler_params=pltpu.CompilerParams(collective_id=0, has_side_effects=True),
    )(send_in, send_up, send_gate, own_in, own_up)


def combine_kernel(
    groups,
    part_out,
    part_back,
    home_out,
    home_back,
    core_in,
    far_out,
    far_in,
    total,
    c_send,
    c_recv,
    y_send,
    y_recv,
    far_send,
    far_recv,
):
    me, h, core_mate, far_mate = places()
    quarter = home_out.shape[2]
    parts = (part_out, part_back)
    homes = (home_out, home_back)
    greet(groups, me, h, core_mate, far_mate)
    far_core_mate = lax.rem(core_mate + 2, 4)
    mate_quarters = (core_mate, far_core_mate)

    def owner_of(d):
        return lax.rem(me + d, groups)

    def core_copy(d, t, which):
        owner = owner_of(d)
        return pltpu.make_async_remote_copy(
            src_ref=parts[t].at[owner, :, columns(mate_quarters[which], quarter)],
            dst_ref=core_in.at[t, which, owner],
            send_sem=c_send.at[t, which, d],
            recv_sem=c_recv.at[t, which, d],
            device_id=(me, core_mate),
            device_id_type=MESH,
        )

    def far_copy(d, t):
        owner = owner_of(d)
        return pltpu.make_async_remote_copy(
            src_ref=far_out.at[t, owner],
            dst_ref=far_in.at[t, owner],
            send_sem=y_send.at[t, d],
            recv_sem=y_recv.at[t, d],
            device_id=(me, far_mate),
            device_id_type=MESH,
        )

    def home_copy(d, t):
        owner = owner_of(d)
        return pltpu.make_async_remote_copy(
            src_ref=total.at[t, owner],
            dst_ref=homes[t].at[me],
            send_sem=far_send.at[t, d],
            recv_sem=far_recv.at[t, d],
            device_id=(owner, h),
            device_id_type=MESH,
        )

    def begin(i, carry):
        d = lax.rem(i + 1, groups)
        for t in range(2):
            for which in (1, 0):
                core_copy(d, t, which).start()
        return carry

    lax.fori_loop(0, groups, begin, 0)

    def first(i):
        d = lax.rem(i + 1, groups)
        owner = owner_of(d)
        for t in range(2):
            core_copy(d, t, 1).wait_recv()
            far_out[t, owner] = (
                parts[t][owner, :, columns(far_mate, quarter)].astype(jnp.float32)
                + core_in[t, 1, owner].astype(jnp.float32)
            ).astype(jnp.bfloat16)
            far_copy(d, t).start()

    def second(i, last):
        d = lax.rem(i + 1, groups)
        owner = owner_of(d)
        for t in range(2):
            core_copy(d, t, 0).wait_recv()
            far_copy(d, t).wait_recv()
            value = (
                parts[t][owner, :, columns(h, quarter)].astype(jnp.float32)
                + core_in[t, 0, owner].astype(jnp.float32)
                + far_in[t, owner].astype(jnp.float32)
            ).astype(jnp.bfloat16)
            if last:
                homes[t][owner] = value
            else:
                total[t, owner] = value
                home_copy(d, t).start()

    first(0)

    def step(i, carry):
        first(i + 1)
        second(i, False)
        return carry

    lax.fori_loop(0, groups - 1, step, 0)
    second(groups - 1, True)

    def finish(i, carry):
        d = lax.rem(i + 1, groups)
        for t in range(2):
            for which in (0, 1):
                core_copy(d, t, which).wait_send()
            far_copy(d, t).wait_send()
        return carry

    lax.fori_loop(0, groups, finish, 0)

    def close(d, carry):
        for t in range(2):
            home_copy(d, t).wait()
        return carry

    lax.fori_loop(1, groups, close, 0)


def combine(groups, part_out, part_back):
    capacity, width = part_out.shape[1:]
    quarter = width // 4
    vmem = pl.BlockSpec(memory_space=pltpu.VMEM)
    dma = pltpu.SemaphoreType.DMA
    block = (groups, capacity, quarter)
    return pl.pallas_call(
        functools.partial(combine_kernel, groups),
        out_shape=(jax.ShapeDtypeStruct(block, jnp.bfloat16),) * 2,
        in_specs=[vmem] * 2,
        out_specs=(vmem,) * 2,
        scratch_shapes=[
            pltpu.VMEM((2, 2) + block, jnp.bfloat16),
            pltpu.VMEM((2,) + block, jnp.bfloat16),
            pltpu.VMEM((2,) + block, jnp.bfloat16),
            pltpu.VMEM((2,) + block, jnp.bfloat16),
            dma((2, 2, groups)),
            dma((2, 2, groups)),
            dma((2, groups)),
            dma((2, groups)),
            dma((2, groups)),
            dma((2, groups)),
        ],
        compiler_params=pltpu.CompilerParams(
            collective_id=1, has_side_effects=True, vmem_limit_bytes=48 * 2**20
        ),
    )(part_out, part_back)


def fused_kernel(
    groups,
    tokens,
    cotangent,
    target_col,
    target_row,
    code_row,
    threshold,
    mask,
    up_any,
    down_any,
    layer_out,
    token_grad,
    grad_up,
    grad_down,
    home_out,
    home_back,
    send_gate,
    level,
    opened,
    cross_buf,
    got_in,
    got_up,
    got_gate,
    send_buf,
    up,
    down,
    gated_all,
    dpre_all,
    part,
    core_in,
    far_out,
    far_in,
    total,
    w_sem,
    far_send,
    far_recv,
    y_send,
    y_recv,
    c_send,
    c_recv,
    r_send,
    r_recv,
    back_c_send,
    back_c_recv,
    back_y_send,
    back_y_recv,
    home_send,
    home_recv,
):
    me, h, core_mate, far_mate = places()
    quarter = home_out.shape[2]
    capacity = home_out.shape[1]
    width = tokens.shape[1]
    hidden_units = down.shape[0]
    slots = groups * capacity
    far_core_mate = lax.rem(core_mate + 2, 4)
    mate_quarters = (core_mate, far_core_mate)
    weight_copies = [
        pltpu.make_async_copy(up_any, up, w_sem.at[0]),
        pltpu.make_async_copy(down_any, down, w_sem.at[1]),
    ]
    for copy in weight_copies:
        copy.start()
    greet(groups, me, h, core_mate, far_mate)
    mine = columns(h, quarter)
    theirs = columns(far_mate, quarter)
    level[...] = threshold[...].astype(jnp.float32) / 64.0
    opened[...] = mask[...].astype(jnp.float32)
    sources = (tokens, cotangent)
    gots = (got_in, got_up)
    homes = (home_out, home_back)

    def remote(src, dst, s_sem, r_sem, device):
        return pltpu.make_async_remote_copy(
            src_ref=src,
            dst_ref=dst,
            send_sem=s_sem,
            recv_sem=r_sem,
            device_id=device,
            device_id_type=MESH,
        )

    def partner(d):
        total_bits, bit = 0, 1
        while bit < groups:
            total_bits = total_bits + lax.rem(me // bit + d // bit, 2) * bit
            bit *= 2
        return total_bits

    def owner_of(d):
        return partner(d)

    def turn(i):
        return lax.rem(3 * i, groups)

    def select(peer):
        rows = lax.broadcasted_iota(jnp.int32, (capacity, tokens.shape[0]), 0) + peer * capacity
        hits = [rows == target_row[k : k + 1, :] for k in range(target_row.shape[0])]
        gate = 0.0
        chosen = 0.0
        for k, hit in enumerate(hits):
            value = code_row[k : k + 1, :].astype(jnp.float32) / 256.0
            gate = gate + jnp.sum(jnp.where(hit, value, 0.0), axis=1, keepdims=True)
            chosen = chosen + jnp.where(hit, 1.0, 0.0)
        spread = jnp.broadcast_to(gate, (capacity, LANES)).astype(jnp.bfloat16)
        return chosen.astype(jnp.bfloat16), spread

    def out_copy(d, t):
        peer = partner(d)
        if t == 2:
            src, dst = send_gate.at[peer], got_gate.at[me]
        else:
            src, dst = send_buf.at[t, peer], gots[t].at[me, :, mine]
        return remote(src, dst, far_send.at[t, d], far_recv.at[t, d], (peer, h))

    def share(d, t, cols, mate, s_sem, r_sem):
        block = gots[t].at[owner_of(d), :, cols]
        return remote(block, block, s_sem.at[t, d], r_sem.at[t, d], (me, mate))

    def y_share(d, t):
        return share(d, t, mine, far_mate, y_send, y_recv)

    def cross_copy(t):
        return remote(
            cross_buf.at[t],
            gots[t].at[me, :, theirs],
            y_send.at[t, 1],
            y_recv.at[t, 1],
            (partner(1), h),
        )

    def core_share(d, t):
        return share(d, t, mine, core_mate, c_send, c_recv)

    def relay_share(d, t):
        return share(d, t, theirs, core_mate, r_send, r_recv)

    def core_copy(d, t, which):
        owner = owner_of(d)
        return remote(
            part.at[t, owner, :, columns(mate_quarters[which], quarter)],
            core_in.at[t, which, owner],
            back_c_send.at[t, which, d],
            back_c_recv.at[t, which, d],
            (me, core_mate),
        )

    def far_copy(d, t):
        owner = owner_of(d)
        return remote(
            far_out.at[t, owner],
            far_in.at[t, owner],
            back_y_send.at[t, d],
            back_y_recv.at[t, d],
            (me, far_mate),
        )

    def home_copy(d, t):
        owner = owner_of(d)
        return remote(
            total.at[t, owner],
            homes[t].at[me],
            home_send.at[t, d],
            home_recv.at[t, d],
            (owner, h),
        )

    def times(a, b):
        return jnp.dot(a, b, preferred_element_type=jnp.float32)

    def times_t(a, b):
        return lax.dot_general(a, b, (((1,), (1,)), ((), ())), preferred_element_type=jnp.float32)

    def t_times(a, b):
        return lax.dot_general(a, b, (((0,), (0,)), ((), ())), preferred_element_type=jnp.float32)

    def begin(i, carry):
        d = turn(i)
        peer = partner(d)
        chosen, spread = select(peer)
        send_gate[peer] = spread
        for t in range(2):
            send_buf[t, peer] = times(chosen, sources[t][:, mine]).astype(jnp.bfloat16)
            out_copy(d, t).start()
        out_copy(d, 2).start()

        @pl.when(d == 1)
        def _():
            for t in range(2):
                cross_buf[t] = times(chosen, sources[t][:, theirs]).astype(jnp.bfloat16)
                cross_copy(t).start()

        return carry

    lax.fori_loop(1, groups, begin, 0)
    own_chosen, own_spread = select(me)
    for t in range(2):
        for q in range(4):
            cols = slice(q * quarter, (q + 1) * quarter)
            gots[t][me, :, cols] = times(own_chosen, sources[t][:, cols]).astype(jnp.bfloat16)
    got_gate[me] = own_spread
    for copy in weight_copies:
        copy.wait()

    def forward(d):
        for t in range(2):
            out_copy(d, t).wait_recv()
            pl.when(d != 1)(lambda: y_share(d, t).start())
            core_share(d, t).start()

    def relay(d):
        for t in range(2):
            pl.when(d != 1)(lambda: y_share(d, t).wait_recv())
            pl.when(d == 1)(lambda: cross_copy(t).wait_recv())
            relay_share(d, t).start()

    def compute(d):
        owner = owner_of(d)
        weight_col = got_gate[owner].astype(jnp.float32)[:, :1]
        pre = times(got_in[owner], up[...])
        sigma = jax.nn.sigmoid(SHARPNESS * (pre - level[...]))
        gated = (weight_col * opened[...] * pre * sigma).astype(jnp.bfloat16)
        back_hidden = times_t(got_up[owner], down[...]) * weight_col
        slope = opened[...] * (sigma + SHARPNESS * pre * sigma * (1.0 - sigma))
        dpre = (back_hidden * slope).astype(jnp.bfloat16)
        gated_all[owner] = gated
        dpre_all[owner] = dpre
        for q in range(4):
            cols = slice(q * quarter, (q + 1) * quarter)
            part[0, owner, :, cols] = times(gated, down[:, cols]).astype(jnp.bfloat16)
            part[1, owner, :, cols] = times_t(dpre, up[cols, :]).astype(jnp.bfloat16)
        for t in range(2):
            for which in (1, 0):
                core_copy(d, t, which).start()

    def compute_arrived(d):
        for t in range(2):
            core_share(d, t).wait_recv()
            relay_share(d, t).wait_recv()
        out_copy(d, 2).wait_recv()
        compute(d)

    def first(d):
        owner = owner_of(d)
        for t in range(2):
            core_copy(d, t, 1).wait_recv()
            far_out[t, owner] = (
                part[t, owner, :, theirs].astype(jnp.float32)
                + core_in[t, 1, owner].astype(jnp.float32)
            ).astype(jnp.bfloat16)
            far_copy(d, t).start()

    def second(d):
        owner = owner_of(d)
        for t in range(2):
            core_copy(d, t, 0).wait_recv()
            far_copy(d, t).wait_recv()
            total[t, owner] = (
                part[t, owner, :, mine].astype(jnp.float32)
                + core_in[t, 0, owner].astype(jnp.float32)
                + far_in[t, owner].astype(jnp.float32)
            ).astype(jnp.bfloat16)

            @pl.when(d > 0)
            def _():
                home_copy(d, t).start()

    compute(0)

    def step(i, carry):
        pl.when(i < groups)(lambda: forward(turn(i)))
        pl.when(i == 1)(lambda: first(0))
        pl.when((i > 1) & (i <= groups))(lambda: relay(turn(i - 1)))
        pl.when(i > 3)(lambda: first(turn(i - 3)))
        pl.when(i > 3)(lambda: second(turn(i - 4)))
        pl.when((i > 2) & (i <= groups + 1))(lambda: compute_arrived(turn(i - 2)))
        return carry

    lax.fori_loop(1, groups + 3, step, 0)
    tile = 512

    def grads(left, right, result, turned):
        def one(n, carry):
            cols = columns(n, tile)
            rows = right[:, :, cols].reshape(slots, tile)
            value = t_times(left[...].reshape(slots, hidden_units), rows)
            if turned:
                result[cols, :] = value.T.astype(jnp.bfloat16)
            else:
                result[:, cols] = value.astype(jnp.bfloat16)
            return carry

        lax.fori_loop(0, width // tile, one, 0)

    grads(gated_all, got_up, grad_down, False)
    second(turn(groups - 1))
    grads(dpre_all, got_in, grad_up, True)
    for t in range(2):
        homes[t][me] = total[t, me]

    def finish(d, carry):
        for t in range(2):
            for which in (0, 1):
                core_copy(d, t, which).wait_send()
            far_copy(d, t).wait_send()

        @pl.when(d > 0)
        def _():
            for t in range(2):
                pl.when(d != 1)(lambda: y_share(d, t).wait_send())
                pl.when(d == 1)(lambda: cross_copy(t).wait_send())
                core_share(d, t).wait_send()
                relay_share(d, t).wait_send()
                home_copy(d, t).wait()
            for t in range(3):
                out_copy(d, t).wait_send()

        return carry

    lax.fori_loop(0, groups, finish, 0)
    lanes = lax.broadcasted_iota(jnp.int32, (tokens.shape[0], slots), 1)
    gather = 0.0
    for k in range(target_col.shape[1]):
        gather = gather + jnp.where(lanes == target_col[:, k : k + 1], 1.0, 0.0)
    gather = gather.astype(jnp.bfloat16)
    for home, result in ((home_out, layer_out), (home_back, token_grad)):
        result[...] = times(gather, home[...].reshape(slots, quarter)).astype(jnp.bfloat16)


def fused(groups, capacity, tokens, cotangent, target, codes, threshold, mask, up_block, down_block):
    width = tokens.shape[1]
    quarter = width // 4
    hidden_units = down_block.shape[0]
    vmem = pl.BlockSpec(memory_space=pltpu.VMEM)
    anywhere = pl.BlockSpec(memory_space=pl.ANY)
    dma = pltpu.SemaphoreType.DMA
    block = (groups, capacity, quarter)
    whole = (groups, capacity, width)
    narrow = (groups, capacity, hidden_units)
    half = jnp.bfloat16
    return pl.pallas_call(
        functools.partial(fused_kernel, groups),
        out_shape=(
            jax.ShapeDtypeStruct((tokens.shape[0], quarter), half),
            jax.ShapeDtypeStruct((tokens.shape[0], quarter), half),
            jax.ShapeDtypeStruct((width, hidden_units), half),
            jax.ShapeDtypeStruct((hidden_units, width), half),
        ),
        in_specs=[vmem] * 7 + [anywhere] * 2,
        out_specs=(vmem,) * 4,
        scratch_shapes=[
            pltpu.VMEM(block, half),
            pltpu.VMEM(block, half),
            pltpu.VMEM((groups, capacity, LANES), half),
            pltpu.VMEM((1, hidden_units), jnp.float32),
            pltpu.VMEM((1, hidden_units), jnp.float32),
            pltpu.VMEM((2, capacity, quarter), half),
            pltpu.VMEM(whole, half),
            pltpu.VMEM(whole, half),
            pltpu.VMEM((groups, capacity, LANES), half),
            pltpu.VMEM((2,) + block, half),
            pltpu.VMEM((width, hidden_units), half),
            pltpu.VMEM((hidden_units, width), half),
            pltpu.VMEM(narrow, half),
            pltpu.VMEM(narrow, half),
            pltpu.VMEM((2,) + whole, half),
            pltpu.VMEM((2, 2) + block, half),
            pltpu.VMEM((2,) + block, half),
            pltpu.VMEM((2,) + block, half),
            pltpu.VMEM((2,) + block, half),
            dma((2,)),
            dma((3, groups)),
            dma((3, groups)),
        ]
        + [dma((2, groups))] * 6
        + [dma((2, 2, groups))] * 2
        + [dma((2, groups))] * 4,
        compiler_params=pltpu.CompilerParams(
            collective_id=2, has_side_effects=True, vmem_limit_bytes=58 * 2**20
        ),
    )(tokens, cotangent, target, target.T, codes.T, threshold, mask, up_block, down_block)


def expert_pass(inputs, upstream, weight_col, up_block, down_block, threshold_row, mask_row):
    pre = jnp.dot(inputs, up_block, preferred_element_type=jnp.float32)
    level = threshold_row.astype(jnp.float32) / 64.0
    opened = mask_row.astype(jnp.float32)
    sigma = jax.nn.sigmoid(SHARPNESS * (pre - level))
    gated = (weight_col * opened * pre * sigma).astype(jnp.bfloat16)
    back_hidden = (
        jnp.einsum("rd,fd->rf", upstream, down_block, preferred_element_type=jnp.float32)
        * weight_col
    )
    slope = opened * (sigma + SHARPNESS * pre * sigma * (1.0 - sigma))
    dpre = (back_hidden * slope).astype(jnp.bfloat16)
    part_out = jnp.dot(gated, down_block, preferred_element_type=jnp.float32)
    part_back = jnp.einsum("rf,df->rd", dpre, up_block, preferred_element_type=jnp.float32)
    grad_down = jnp.einsum("rf,rd->fd", gated, upstream, preferred_element_type=jnp.float32).astype(
        jnp.bfloat16
    )
    grad_up = jnp.einsum("rd,rf->df", inputs, dpre, preferred_element_type=jnp.float32).astype(
        jnp.bfloat16
    )
    return (part_out, part_back, grad_up, grad_down)


def shards(
    tokens, cotangent, expert_ids, gate_codes, up_weight, down_weight, threshold_state, spike_mask
):
    groups = lax.axis_size("expert")
    me = lax.axis_index("expert")
    h = lax.axis_index("hidden")
    tok_rows, width = tokens.shape
    quarter = width // lax.axis_size("hidden")
    top = expert_ids.shape[1]
    capacity = 4 * tok_rows // groups
    pairs = tok_rows * top
    slots = groups * capacity
    flat_ids = expert_ids.reshape(pairs)
    pair_index = jnp.arange(pairs, dtype=jnp.int32)
    earlier = (flat_ids[None, :] == flat_ids[:, None]) & (pair_index[None, :] < pair_index[:, None])
    place = jnp.sum(earlier.astype(jnp.int32), axis=1)
    target = (flat_ids * capacity + place).reshape(tok_rows, top)
    if capacity % 16 == 0 and groups & (groups - 1) == 0:
        layer_out, token_grad, grad_up, grad_down = fused(
            groups,
            capacity,
            tokens,
            cotangent,
            target,
            gate_codes,
            threshold_state,
            spike_mask,
            up_weight[0],
            down_weight[0],
        )
        return (layer_out, token_grad, grad_up[None], grad_down[None])
    slot_index = jnp.arange(slots, dtype=jnp.int32)
    gates = gate_codes.astype(jnp.float32) / 256.0
    hits = [target[None, :, k] == slot_index[:, None] for k in range(top)]
    pick = functools.reduce(jnp.logical_or, hits).astype(jnp.bfloat16)
    slot_gate = sum(
        jnp.sum(jnp.where(hits[k], gates[None, :, k], 0.0), axis=1) for k in range(top)
    ).astype(jnp.bfloat16)
    send_gate = jnp.broadcast_to(slot_gate[:, None], (slots, LANES)).reshape(
        groups, capacity, LANES
    )

    def choose(which, rows):
        return jnp.dot(which, rows, preferred_element_type=jnp.float32).astype(jnp.bfloat16)

    own_pick = lax.dynamic_slice_in_dim(pick, me * capacity, capacity, 0)
    tok_cut = lax.dynamic_slice_in_dim(tokens, h * quarter, quarter, 1)
    cot_cut = lax.dynamic_slice_in_dim(cotangent, h * quarter, quarter, 1)
    got_in, got_up, got_gate = dispatch(
        groups,
        choose(pick, tok_cut).reshape(groups, capacity, quarter),
        choose(pick, cot_cut).reshape(groups, capacity, quarter),
        send_gate,
        choose(own_pick, tokens),
        choose(own_pick, cotangent),
    )
    part_out, part_back, grad_up, grad_down = expert_pass(
        got_in.reshape(slots, width),
        got_up.reshape(slots, width),
        got_gate.reshape(slots, LANES)[:, :1].astype(jnp.float32),
        up_weight[0],
        down_weight[0],
        threshold_state[0],
        spike_mask[0],
    )
    home_out, home_back = combine(
        groups,
        part_out.astype(jnp.bfloat16).reshape(groups, capacity, width),
        part_back.astype(jnp.bfloat16).reshape(groups, capacity, width),
    )

    def gather_home(home):
        return jnp.einsum(
            "st,sw->tw", pick, home.reshape(slots, quarter), preferred_element_type=jnp.float32
        ).astype(jnp.bfloat16)

    return (gather_home(home_out), gather_home(home_back), grad_up[None], grad_down[None])


def solution(mesh):
    placed = (
        P("expert", None),
        P("expert", None),
        P("expert", None),
        P("expert", None),
        P("expert", None, "hidden"),
        P("expert", "hidden", None),
        P("expert", "hidden"),
        P("expert", "hidden"),
    )
    return jax.shard_map(
        shards,
        mesh=mesh,
        in_specs=placed,
        out_specs=(
            P("expert", "hidden"),
            P("expert", "hidden"),
            P("expert", None, "hidden"),
            P("expert", "hidden", None),
        ),
        check_vma=False,
    )
```

```python
import functools

import jax
import jax.numpy as jnp
from jax import lax
from jax.experimental import pallas as pl
from jax.experimental.pallas import tpu as pltpu
from jax.sharding import PartitionSpec as P

SHARPNESS = 2.0
LANES = 128
MESH = pl.DeviceIdType.MESH


def greet(groups, me, h, core_mate, far_mate):
    barrier = pltpu.get_barrier_semaphore()

    def hello(d, carry):
        peer = lax.rem(me + d, groups)
        pl.semaphore_signal(barrier, inc=1, device_id=(peer, h), device_id_type=MESH)
        return carry

    lax.fori_loop(1, groups, hello, 0)
    for mate in (core_mate, far_mate):
        pl.semaphore_signal(barrier, inc=1, device_id=(me, mate), device_id_type=MESH)
    pl.semaphore_wait(barrier, groups + 1)


def places():
    me = lax.axis_index("expert")
    h = lax.axis_index("hidden")
    core_mate = h + 1 - 2 * lax.rem(h, 2)
    far_mate = lax.rem(h + 2, 4)
    return me, h, core_mate, far_mate


def columns(index, width):
    return pl.ds(pl.multiple_of(index * width, width), width)


def dispatch_kernel(
    groups,
    send_in,
    send_up,
    send_gate,
    own_in,
    own_up,
    got_in,
    got_up,
    got_gate,
    far_send,
    far_recv,
    y_send,
    y_recv,
    c_send,
    c_recv,
    r_send,
    r_recv,
    own_sem,
):
    me, h, core_mate, far_mate = places()
    quarter = send_in.shape[2]
    greet(groups, me, h, core_mate, far_mate)
    mine = columns(h, quarter)
    theirs = columns(far_mate, quarter)
    tensors = ((send_in, got_in, own_in), (send_up, got_up, own_up))

    def out_copies(d):
        peer = lax.rem(me + d, groups)
        made = [
            pltpu.make_async_remote_copy(
                src_ref=src.at[peer],
                dst_ref=dst.at[me, :, mine],
                send_sem=far_send.at[t, d],
                recv_sem=far_recv.at[t, d],
                device_id=(peer, h),
                device_id_type=MESH,
            )
            for t, (src, dst, own) in enumerate(tensors)
        ]
        made.append(
            pltpu.make_async_remote_copy(
                src_ref=send_gate.at[peer],
                dst_ref=got_gate.at[me],
                send_sem=far_send.at[2, d],
                recv_sem=far_recv.at[2, d],
                device_id=(peer, h),
                device_id_type=MESH,
            )
        )
        return made

    def share(d, t, cols, mate, s_sem, r_sem):
        owner = lax.rem(me + groups - d, groups)
        block = tensors[t][1].at[owner, :, cols]
        return pltpu.make_async_remote_copy(
            src_ref=block,
            dst_ref=block,
            send_sem=s_sem.at[t, d],
            recv_sem=r_sem.at[t, d],
            device_id=(me, mate),
            device_id_type=MESH,
        )

    def begin(d, carry):
        for copy in out_copies(d):
            copy.start()
        return carry

    lax.fori_loop(1, groups, begin, 0)
    own_copies = [
        pltpu.make_async_copy(own_in, got_in.at[me], own_sem.at[0]),
        pltpu.make_async_copy(own_up, got_up.at[me], own_sem.at[1]),
        pltpu.make_async_copy(send_gate.at[me], got_gate.at[me], own_sem.at[2]),
    ]
    for copy in own_copies:
        copy.start()

    def relay(d):
        for t in range(2):
            share(d, t, mine, far_mate, y_send, y_recv).wait_recv()
            share(d, t, theirs, core_mate, r_send, r_recv).start()

    def forward(d, carry):
        arrived = out_copies(d)
        for t in range(2):
            arrived[t].wait_recv()
            share(d, t, mine, far_mate, y_send, y_recv).start()
            share(d, t, mine, core_mate, c_send, c_recv).start()

        @pl.when(d > 1)
        def _():
            relay(d - 1)

        return carry

    lax.fori_loop(1, groups, forward, 0)
    relay(groups - 1)

    def finish(d, carry):
        for copy in out_copies(d):
            copy.wait_send()
        out_copies(d)[2].wait_recv()
        for t in range(2):
            share(d, t, mine, far_mate, y_send, y_recv).wait_send()
            share(d, t, mine, core_mate, c_send, c_recv).wait()
            share(d, t, theirs, core_mate, r_send, r_recv).wait()
        return carry

    lax.fori_loop(1, groups, finish, 0)
    for copy in own_copies:
        copy.wait()


def dispatch(groups, send_in, send_up, send_gate, own_in, own_up):
    capacity, quarter = send_in.shape[1:]
    width = own_in.shape[1]
    anywhere = pl.BlockSpec(memory_space=pl.ANY)
    dma = pltpu.SemaphoreType.DMA
    return pl.pallas_call(
        functools.partial(dispatch_kernel, groups),
        out_shape=(
            jax.ShapeDtypeStruct((groups, capacity, width), jnp.bfloat16),
            jax.ShapeDtypeStruct((groups, capacity, width), jnp.bfloat16),
            jax.ShapeDtypeStruct((groups, capacity, LANES), jnp.bfloat16),
        ),
        in_specs=[anywhere] * 5,
        out_specs=(anywhere,) * 3,
        scratch_shapes=[dma((3, groups)), dma((3, groups))]
        + [dma((2, groups))] * 6
        + [dma((3,))],
        compiler_params=pltpu.CompilerParams(collective_id=0, has_side_effects=True),
    )(send_in, send_up, send_gate, own_in, own_up)


def combine_kernel(
    groups,
    part_out,
    part_back,
    home_out,
    home_back,
    core_in,
    far_out,
    far_in,
    total,
    c_send,
    c_recv,
    y_send,
    y_recv,
    far_send,
    far_recv,
):
    me, h, core_mate, far_mate = places()
    quarter = home_out.shape[2]
    parts = (part_out, part_back)
    homes = (home_out, home_back)
    greet(groups, me, h, core_mate, far_mate)
    far_core_mate = lax.rem(core_mate + 2, 4)
    mate_quarters = (core_mate, far_core_mate)

    def owner_of(d):
        return lax.rem(me + d, groups)

    def core_copy(d, t, which):
        owner = owner_of(d)
        return pltpu.make_async_remote_copy(
            src_ref=parts[t].at[owner, :, columns(mate_quarters[which], quarter)],
            dst_ref=core_in.at[t, which, owner],
            send_sem=c_send.at[t, which, d],
            recv_sem=c_recv.at[t, which, d],
            device_id=(me, core_mate),
            device_id_type=MESH,
        )

    def far_copy(d, t):
        owner = owner_of(d)
        return pltpu.make_async_remote_copy(
            src_ref=far_out.at[t, owner],
            dst_ref=far_in.at[t, owner],
            send_sem=y_send.at[t, d],
            recv_sem=y_recv.at[t, d],
            device_id=(me, far_mate),
            device_id_type=MESH,
        )

    def home_copy(d, t):
        owner = owner_of(d)
        return pltpu.make_async_remote_copy(
            src_ref=total.at[t, owner],
            dst_ref=homes[t].at[me],
            send_sem=far_send.at[t, d],
            recv_sem=far_recv.at[t, d],
            device_id=(owner, h),
            device_id_type=MESH,
        )

    def begin(i, carry):
        d = lax.rem(i + 1, groups)
        for t in range(2):
            for which in (1, 0):
                core_copy(d, t, which).start()
        return carry

    lax.fori_loop(0, groups, begin, 0)

    def first(i):
        d = lax.rem(i + 1, groups)
        owner = owner_of(d)
        for t in range(2):
            core_copy(d, t, 1).wait_recv()
            far_out[t, owner] = (
                parts[t][owner, :, columns(far_mate, quarter)].astype(jnp.float32)
                + core_in[t, 1, owner].astype(jnp.float32)
            ).astype(jnp.bfloat16)
            far_copy(d, t).start()

    def second(i, last):
        d = lax.rem(i + 1, groups)
        owner = owner_of(d)
        for t in range(2):
            core_copy(d, t, 0).wait_recv()
            far_copy(d, t).wait_recv()
            value = (
                parts[t][owner, :, columns(h, quarter)].astype(jnp.float32)
                + core_in[t, 0, owner].astype(jnp.float32)
                + far_in[t, owner].astype(jnp.float32)
            ).astype(jnp.bfloat16)
            if last:
                homes[t][owner] = value
            else:
                total[t, owner] = value
                home_copy(d, t).start()

    first(0)

    def step(i, carry):
        first(i + 1)
        second(i, False)
        return carry

    lax.fori_loop(0, groups - 1, step, 0)
    second(groups - 1, True)

    def finish(i, carry):
        d = lax.rem(i + 1, groups)
        for t in range(2):
            for which in (0, 1):
                core_copy(d, t, which).wait_send()
            far_copy(d, t).wait_send()
        return carry

    lax.fori_loop(0, groups, finish, 0)

    def close(d, carry):
        for t in range(2):
            home_copy(d, t).wait()
        return carry

    lax.fori_loop(1, groups, close, 0)


def combine(groups, part_out, part_back):
    capacity, width = part_out.shape[1:]
    quarter = width // 4
    vmem = pl.BlockSpec(memory_space=pltpu.VMEM)
    dma = pltpu.SemaphoreType.DMA
    block = (groups, capacity, quarter)
    return pl.pallas_call(
        functools.partial(combine_kernel, groups),
        out_shape=(jax.ShapeDtypeStruct(block, jnp.bfloat16),) * 2,
        in_specs=[vmem] * 2,
        out_specs=(vmem,) * 2,
        scratch_shapes=[
            pltpu.VMEM((2, 2) + block, jnp.bfloat16),
            pltpu.VMEM((2,) + block, jnp.bfloat16),
            pltpu.VMEM((2,) + block, jnp.bfloat16),
            pltpu.VMEM((2,) + block, jnp.bfloat16),
            dma((2, 2, groups)),
            dma((2, 2, groups)),
            dma((2, groups)),
            dma((2, groups)),
            dma((2, groups)),
            dma((2, groups)),
        ],
        compiler_params=pltpu.CompilerParams(
            collective_id=1, has_side_effects=True, vmem_limit_bytes=48 * 2**20
        ),
    )(part_out, part_back)


def fused_kernel(
    groups,
    tokens,
    cotangent,
    target_col,
    target_row,
    code_row,
    threshold,
    mask,
    up_any,
    down_any,
    layer_out,
    token_grad,
    grad_up,
    grad_down,
    home_out,
    home_back,
    send_gate,
    level,
    opened,
    cross_buf,
    got_in,
    got_up,
    got_gate,
    send_buf,
    up,
    down,
    gated_all,
    dpre_all,
    part,
    core_in,
    far_out,
    far_in,
    total,
    w_sem,
    far_send,
    far_recv,
    y_send,
    y_recv,
    c_send,
    c_recv,
    r_send,
    r_recv,
    back_c_send,
    back_c_recv,
    back_y_send,
    back_y_recv,
    home_send,
    home_recv,
):
    me, h, core_mate, far_mate = places()
    quarter = home_out.shape[2]
    capacity = home_out.shape[1]
    width = tokens.shape[1]
    hidden_units = down.shape[0]
    slots = groups * capacity
    far_core_mate = lax.rem(core_mate + 2, 4)
    mate_quarters = (core_mate, far_core_mate)
    weight_copies = [
        pltpu.make_async_copy(up_any, up, w_sem.at[0]),
        pltpu.make_async_copy(down_any, down, w_sem.at[1]),
    ]
    for copy in weight_copies:
        copy.start()
    greet(groups, me, h, core_mate, far_mate)
    mine = columns(h, quarter)
    theirs = columns(far_mate, quarter)
    level[...] = threshold[...].astype(jnp.float32) / 64.0
    opened[...] = mask[...].astype(jnp.float32)
    sources = (tokens, cotangent)
    gots = (got_in, got_up)
    homes = (home_out, home_back)

    def remote(src, dst, s_sem, r_sem, device):
        return pltpu.make_async_remote_copy(
            src_ref=src,
            dst_ref=dst,
            send_sem=s_sem,
            recv_sem=r_sem,
            device_id=device,
            device_id_type=MESH,
        )

    def partner(d):
        total_bits, bit = 0, 1
        while bit < groups:
            total_bits = total_bits + lax.rem(me // bit + d // bit, 2) * bit
            bit *= 2
        return total_bits

    def owner_of(d):
        return partner(d)

    def turn(i):
        return lax.rem(5 * i, groups)

    def select(peer):
        rows = lax.broadcasted_iota(jnp.int32, (capacity, tokens.shape[0]), 0) + peer * capacity
        hits = [rows == target_row[k : k + 1, :] for k in range(target_row.shape[0])]
        gate = 0.0
        chosen = 0.0
        for k, hit in enumerate(hits):
            value = code_row[k : k + 1, :].astype(jnp.float32) / 256.0
            gate = gate + jnp.sum(jnp.where(hit, value, 0.0), axis=1, keepdims=True)
            chosen = chosen + jnp.where(hit, 1.0, 0.0)
        spread = jnp.broadcast_to(gate, (capacity, LANES)).astype(jnp.bfloat16)
        return chosen.astype(jnp.bfloat16), spread

    def out_copy(d, t):
        peer = partner(d)
        if t == 2:
            src, dst = send_gate.at[peer], got_gate.at[me]
        else:
            src, dst = send_buf.at[t, peer], gots[t].at[me, :, mine]
        return remote(src, dst, far_send.at[t, d], far_recv.at[t, d], (peer, h))

    def share(d, t, cols, mate, s_sem, r_sem):
        block = gots[t].at[owner_of(d), :, cols]
        return remote(block, block, s_sem.at[t, d], r_sem.at[t, d], (me, mate))

    def y_share(d, t):
        return share(d, t, mine, far_mate, y_send, y_recv)

    def cross_copy(t):
        return remote(
            cross_buf.at[t],
            gots[t].at[me, :, theirs],
            y_send.at[t, 1],
            y_recv.at[t, 1],
            (partner(1), h),
        )

    def core_share(d, t):
        return share(d, t, mine, core_mate, c_send, c_recv)

    def relay_share(d, t):
        return share(d, t, theirs, core_mate, r_send, r_recv)

    def core_copy(d, t, which):
        owner = owner_of(d)
        return remote(
            part.at[t, owner, :, columns(mate_quarters[which], quarter)],
            core_in.at[t, which, owner],
            back_c_send.at[t, which, d],
            back_c_recv.at[t, which, d],
            (me, core_mate),
        )

    def far_copy(d, t):
        owner = owner_of(d)
        return remote(
            far_out.at[t, owner],
            far_in.at[t, owner],
            back_y_send.at[t, d],
            back_y_recv.at[t, d],
            (me, far_mate),
        )

    def home_copy(d, t):
        owner = owner_of(d)
        return remote(
            total.at[t, owner],
            homes[t].at[me],
            home_send.at[t, d],
            home_recv.at[t, d],
            (owner, h),
        )

    def times(a, b):
        return jnp.dot(a, b, preferred_element_type=jnp.float32)

    def times_t(a, b):
        return lax.dot_general(a, b, (((1,), (1,)), ((), ())), preferred_element_type=jnp.float32)

    def t_times(a, b):
        return lax.dot_general(a, b, (((0,), (0,)), ((), ())), preferred_element_type=jnp.float32)

    def begin(i, carry):
        d = turn(i)
        peer = partner(d)
        chosen, spread = select(peer)
        send_gate[peer] = spread
        for t in range(2):
            send_buf[t, peer] = times(chosen, sources[t][:, mine]).astype(jnp.bfloat16)
            out_copy(d, t).start()
        out_copy(d, 2).start()

        @pl.when(d == 1)
        def _():
            for t in range(2):
                cross_buf[t] = times(chosen, sources[t][:, theirs]).astype(jnp.bfloat16)
                cross_copy(t).start()

        return carry

    lax.fori_loop(1, groups, begin, 0)
    own_chosen, own_spread = select(me)
    for t in range(2):
        for q in range(4):
            cols = slice(q * quarter, (q + 1) * quarter)
            gots[t][me, :, cols] = times(own_chosen, sources[t][:, cols]).astype(jnp.bfloat16)
    got_gate[me] = own_spread
    for copy in weight_copies:
        copy.wait()

    def forward(d):
        for t in range(2):
            out_copy(d, t).wait_recv()
            pl.when(d != 1)(lambda: y_share(d, t).start())
            core_share(d, t).start()

    def relay(d):
        for t in range(2):
            pl.when(d != 1)(lambda: y_share(d, t).wait_recv())
            pl.when(d == 1)(lambda: cross_copy(t).wait_recv())
            relay_share(d, t).start()

    def compute(d):
        owner = owner_of(d)
        weight_col = got_gate[owner].astype(jnp.float32)[:, :1]
        pre = times(got_in[owner], up[...])
        sigma = jax.nn.sigmoid(SHARPNESS * (pre - level[...]))
        gated = (weight_col * opened[...] * pre * sigma).astype(jnp.bfloat16)
        back_hidden = times_t(got_up[owner], down[...]) * weight_col
        slope = opened[...] * (sigma + SHARPNESS * pre * sigma * (1.0 - sigma))
        dpre = (back_hidden * slope).astype(jnp.bfloat16)
        gated_all[owner] = gated
        dpre_all[owner] = dpre
        for q in range(4):
            cols = slice(q * quarter, (q + 1) * quarter)
            part[0, owner, :, cols] = times(gated, down[:, cols]).astype(jnp.bfloat16)
            part[1, owner, :, cols] = times_t(dpre, up[cols, :]).astype(jnp.bfloat16)
        for t in range(2):
            for which in (1, 0):
                core_copy(d, t, which).start()

    def compute_arrived(d):
        for t in range(2):
            core_share(d, t).wait_recv()
            relay_share(d, t).wait_recv()
        out_copy(d, 2).wait_recv()
        compute(d)

    def first(d):
        owner = owner_of(d)
        for t in range(2):
            core_copy(d, t, 1).wait_recv()
            far_out[t, owner] = (
                part[t, owner, :, theirs].astype(jnp.float32)
                + core_in[t, 1, owner].astype(jnp.float32)
            ).astype(jnp.bfloat16)
            far_copy(d, t).start()

    def second(d):
        owner = owner_of(d)
        for t in range(2):
            core_copy(d, t, 0).wait_recv()
            far_copy(d, t).wait_recv()
            total[t, owner] = (
                part[t, owner, :, mine].astype(jnp.float32)
                + core_in[t, 0, owner].astype(jnp.float32)
                + far_in[t, owner].astype(jnp.float32)
            ).astype(jnp.bfloat16)

            @pl.when(d > 0)
            def _():
                home_copy(d, t).start()

    compute(0)

    def step(i, carry):
        pl.when(i < groups)(lambda: forward(turn(i)))
        pl.when(i == 1)(lambda: first(0))
        pl.when((i > 1) & (i <= groups))(lambda: relay(turn(i - 1)))
        pl.when(i > 3)(lambda: first(turn(i - 3)))
        pl.when(i > 3)(lambda: second(turn(i - 4)))
        pl.when((i > 2) & (i <= groups + 1))(lambda: compute_arrived(turn(i - 2)))
        return carry

    lax.fori_loop(1, groups + 3, step, 0)
    tile = 512

    def grads(left, right, result, turned):
        def one(n, carry):
            cols = columns(n, tile)
            rows = right[:, :, cols].reshape(slots, tile)
            value = t_times(left[...].reshape(slots, hidden_units), rows)
            if turned:
                result[cols, :] = value.T.astype(jnp.bfloat16)
            else:
                result[:, cols] = value.astype(jnp.bfloat16)
            return carry

        lax.fori_loop(0, width // tile, one, 0)

    grads(gated_all, got_up, grad_down, False)
    second(turn(groups - 1))
    grads(dpre_all, got_in, grad_up, True)
    for t in range(2):
        homes[t][me] = total[t, me]

    def finish(d, carry):
        for t in range(2):
            for which in (0, 1):
                core_copy(d, t, which).wait_send()
            far_copy(d, t).wait_send()

        @pl.when(d > 0)
        def _():
            for t in range(2):
                pl.when(d != 1)(lambda: y_share(d, t).wait_send())
                pl.when(d == 1)(lambda: cross_copy(t).wait_send())
                core_share(d, t).wait_send()
                relay_share(d, t).wait_send()
                home_copy(d, t).wait()
            for t in range(3):
                out_copy(d, t).wait_send()

        return carry

    lax.fori_loop(0, groups, finish, 0)
    lanes = lax.broadcasted_iota(jnp.int32, (tokens.shape[0], slots), 1)
    gather = 0.0
    for k in range(target_col.shape[1]):
        gather = gather + jnp.where(lanes == target_col[:, k : k + 1], 1.0, 0.0)
    gather = gather.astype(jnp.bfloat16)
    for home, result in ((home_out, layer_out), (home_back, token_grad)):
        result[...] = times(gather, home[...].reshape(slots, quarter)).astype(jnp.bfloat16)


def write_kernel(*refs):
    half = (len(refs) - 1) // 2
    sems = refs[-1]
    copies = [
        pltpu.make_async_copy(refs[i], refs[half + i], sems.at[i]) for i in range(half)
    ]
    for copy in copies:
        copy.start()
    for copy in copies:
        copy.wait()


def write_out(results):
    anywhere = pl.BlockSpec(memory_space=pl.ANY)
    return pl.pallas_call(
        write_kernel,
        out_shape=tuple(jax.ShapeDtypeStruct(r.shape, r.dtype) for r in results),
        in_specs=[anywhere] * len(results),
        out_specs=(anywhere,) * len(results),
        scratch_shapes=[pltpu.SemaphoreType.DMA((len(results),))],
    )(*results)


def fused(groups, capacity, tokens, cotangent, target, codes, threshold, mask, up_block, down_block):
    width = tokens.shape[1]
    quarter = width // 4
    hidden_units = down_block.shape[0]
    vmem = pl.BlockSpec(memory_space=pltpu.VMEM)
    anywhere = pl.BlockSpec(memory_space=pl.ANY)
    dma = pltpu.SemaphoreType.DMA
    block = (groups, capacity, quarter)
    whole = (groups, capacity, width)
    narrow = (groups, capacity, hidden_units)
    half = jnp.bfloat16
    return pl.pallas_call(
        functools.partial(fused_kernel, groups),
        out_shape=(
            jax.ShapeDtypeStruct((tokens.shape[0], quarter), half),
            jax.ShapeDtypeStruct((tokens.shape[0], quarter), half),
            jax.ShapeDtypeStruct((width, hidden_units), half),
            jax.ShapeDtypeStruct((hidden_units, width), half),
        ),
        in_specs=[vmem] * 7 + [anywhere] * 2,
        out_specs=(vmem,) * 4,
        scratch_shapes=[
            pltpu.VMEM(block, half),
            pltpu.VMEM(block, half),
            pltpu.VMEM((groups, capacity, LANES), half),
            pltpu.VMEM((1, hidden_units), jnp.float32),
            pltpu.VMEM((1, hidden_units), jnp.float32),
            pltpu.VMEM((2, capacity, quarter), half),
            pltpu.VMEM(whole, half),
            pltpu.VMEM(whole, half),
            pltpu.VMEM((groups, capacity, LANES), half),
            pltpu.VMEM((2,) + block, half),
            pltpu.VMEM((width, hidden_units), half),
            pltpu.VMEM((hidden_units, width), half),
            pltpu.VMEM(narrow, half),
            pltpu.VMEM(narrow, half),
            pltpu.VMEM((2,) + whole, half),
            pltpu.VMEM((2, 2) + block, half),
            pltpu.VMEM((2,) + block, half),
            pltpu.VMEM((2,) + block, half),
            pltpu.VMEM((2,) + block, half),
            dma((2,)),
            dma((3, groups)),
            dma((3, groups)),
        ]
        + [dma((2, groups))] * 6
        + [dma((2, 2, groups))] * 2
        + [dma((2, groups))] * 4,
        compiler_params=pltpu.CompilerParams(
            collective_id=2, has_side_effects=True, vmem_limit_bytes=58 * 2**20
        ),
    )(tokens, cotangent, target, target.T, codes.T, threshold, mask, up_block, down_block)


def expert_pass(inputs, upstream, weight_col, up_block, down_block, threshold_row, mask_row):
    pre = jnp.dot(inputs, up_block, preferred_element_type=jnp.float32)
    level = threshold_row.astype(jnp.float32) / 64.0
    opened = mask_row.astype(jnp.float32)
    sigma = jax.nn.sigmoid(SHARPNESS * (pre - level))
    gated = (weight_col * opened * pre * sigma).astype(jnp.bfloat16)
    back_hidden = (
        jnp.einsum("rd,fd->rf", upstream, down_block, preferred_element_type=jnp.float32)
        * weight_col
    )
    slope = opened * (sigma + SHARPNESS * pre * sigma * (1.0 - sigma))
    dpre = (back_hidden * slope).astype(jnp.bfloat16)
    part_out = jnp.dot(gated, down_block, preferred_element_type=jnp.float32)
    part_back = jnp.einsum("rf,df->rd", dpre, up_block, preferred_element_type=jnp.float32)
    grad_down = jnp.einsum("rf,rd->fd", gated, upstream, preferred_element_type=jnp.float32).astype(
        jnp.bfloat16
    )
    grad_up = jnp.einsum("rd,rf->df", inputs, dpre, preferred_element_type=jnp.float32).astype(
        jnp.bfloat16
    )
    return (part_out, part_back, grad_up, grad_down)


def shards(
    tokens, cotangent, expert_ids, gate_codes, up_weight, down_weight, threshold_state, spike_mask
):
    groups = lax.axis_size("expert")
    me = lax.axis_index("expert")
    h = lax.axis_index("hidden")
    tok_rows, width = tokens.shape
    quarter = width // lax.axis_size("hidden")
    top = expert_ids.shape[1]
    capacity = 4 * tok_rows // groups
    pairs = tok_rows * top
    slots = groups * capacity
    flat_ids = expert_ids.reshape(pairs)
    pair_index = jnp.arange(pairs, dtype=jnp.int32)
    earlier = (flat_ids[None, :] == flat_ids[:, None]) & (pair_index[None, :] < pair_index[:, None])
    place = jnp.sum(earlier.astype(jnp.int32), axis=1)
    target = (flat_ids * capacity + place).reshape(tok_rows, top)
    if capacity % 16 == 0 and groups & (groups - 1) == 0:
        results = fused(
            groups,
            capacity,
            tokens,
            cotangent,
            target,
            gate_codes,
            threshold_state,
            spike_mask,
            up_weight[0],
            down_weight[0],
        )
        layer_out, token_grad, grad_up, grad_down = write_out(results)
        return (layer_out, token_grad, grad_up[None], grad_down[None])
    slot_index = jnp.arange(slots, dtype=jnp.int32)
    gates = gate_codes.astype(jnp.float32) / 256.0
    hits = [target[None, :, k] == slot_index[:, None] for k in range(top)]
    pick = functools.reduce(jnp.logical_or, hits).astype(jnp.bfloat16)
    slot_gate = sum(
        jnp.sum(jnp.where(hits[k], gates[None, :, k], 0.0), axis=1) for k in range(top)
    ).astype(jnp.bfloat16)
    send_gate = jnp.broadcast_to(slot_gate[:, None], (slots, LANES)).reshape(
        groups, capacity, LANES
    )

    def choose(which, rows):
        return jnp.dot(which, rows, preferred_element_type=jnp.float32).astype(jnp.bfloat16)

    own_pick = lax.dynamic_slice_in_dim(pick, me * capacity, capacity, 0)
    tok_cut = lax.dynamic_slice_in_dim(tokens, h * quarter, quarter, 1)
    cot_cut = lax.dynamic_slice_in_dim(cotangent, h * quarter, quarter, 1)
    got_in, got_up, got_gate = dispatch(
        groups,
        choose(pick, tok_cut).reshape(groups, capacity, quarter),
        choose(pick, cot_cut).reshape(groups, capacity, quarter),
        send_gate,
        choose(own_pick, tokens),
        choose(own_pick, cotangent),
    )
    part_out, part_back, grad_up, grad_down = expert_pass(
        got_in.reshape(slots, width),
        got_up.reshape(slots, width),
        got_gate.reshape(slots, LANES)[:, :1].astype(jnp.float32),
        up_weight[0],
        down_weight[0],
        threshold_state[0],
        spike_mask[0],
    )
    home_out, home_back = combine(
        groups,
        part_out.astype(jnp.bfloat16).reshape(groups, capacity, width),
        part_back.astype(jnp.bfloat16).reshape(groups, capacity, width),
    )

    def gather_home(home):
        return jnp.einsum(
            "st,sw->tw", pick, home.reshape(slots, quarter), preferred_element_type=jnp.float32
        ).astype(jnp.bfloat16)

    return (gather_home(home_out), gather_home(home_back), grad_up[None], grad_down[None])


def solution(mesh):
    placed = (
        P("expert", None),
        P("expert", None),
        P("expert", None),
        P("expert", None),
        P("expert", None, "hidden"),
        P("expert", "hidden", None),
        P("expert", "hidden"),
        P("expert", "hidden"),
    )
    return jax.shard_map(
        shards,
        mesh=mesh,
        in_specs=placed,
        out_specs=(
            P("expert", "hidden"),
            P("expert", "hidden"),
            P("expert", None, "hidden"),
            P("expert", "hidden", None),
        ),
        check_vma=False,
    )
```

```python
import functools

import jax
import jax.numpy as jnp
from jax import lax
from jax.experimental import pallas as pl
from jax.experimental.pallas import tpu as pltpu
from jax.sharding import PartitionSpec as P

SHARPNESS = 2.0
LANES = 128
MESH = pl.DeviceIdType.MESH


def greet(groups, me, h, core_mate, far_mate):
    barrier = pltpu.get_barrier_semaphore()

    def hello(d, carry):
        peer = lax.rem(me + d, groups)
        pl.semaphore_signal(barrier, inc=1, device_id=(peer, h), device_id_type=MESH)
        return carry

    lax.fori_loop(1, groups, hello, 0)
    for mate in (core_mate, far_mate):
        pl.semaphore_signal(barrier, inc=1, device_id=(me, mate), device_id_type=MESH)
    pl.semaphore_wait(barrier, groups + 1)


def places():
    me = lax.axis_index("expert")
    h = lax.axis_index("hidden")
    core_mate = h + 1 - 2 * lax.rem(h, 2)
    far_mate = lax.rem(h + 2, 4)
    return me, h, core_mate, far_mate


def columns(index, width):
    return pl.ds(pl.multiple_of(index * width, width), width)


def dispatch_kernel(
    groups,
    send_in,
    send_up,
    send_gate,
    own_in,
    own_up,
    got_in,
    got_up,
    got_gate,
    far_send,
    far_recv,
    y_send,
    y_recv,
    c_send,
    c_recv,
    r_send,
    r_recv,
    own_sem,
):
    me, h, core_mate, far_mate = places()
    quarter = send_in.shape[2]
    greet(groups, me, h, core_mate, far_mate)
    mine = columns(h, quarter)
    theirs = columns(far_mate, quarter)
    tensors = ((send_in, got_in, own_in), (send_up, got_up, own_up))

    def out_copies(d):
        peer = lax.rem(me + d, groups)
        made = [
            pltpu.make_async_remote_copy(
                src_ref=src.at[peer],
                dst_ref=dst.at[me, :, mine],
                send_sem=far_send.at[t, d],
                recv_sem=far_recv.at[t, d],
                device_id=(peer, h),
                device_id_type=MESH,
            )
            for t, (src, dst, own) in enumerate(tensors)
        ]
        made.append(
            pltpu.make_async_remote_copy(
                src_ref=send_gate.at[peer],
                dst_ref=got_gate.at[me],
                send_sem=far_send.at[2, d],
                recv_sem=far_recv.at[2, d],
                device_id=(peer, h),
                device_id_type=MESH,
            )
        )
        return made

    def share(d, t, cols, mate, s_sem, r_sem):
        owner = lax.rem(me + groups - d, groups)
        block = tensors[t][1].at[owner, :, cols]
        return pltpu.make_async_remote_copy(
            src_ref=block,
            dst_ref=block,
            send_sem=s_sem.at[t, d],
            recv_sem=r_sem.at[t, d],
            device_id=(me, mate),
            device_id_type=MESH,
        )

    def begin(d, carry):
        for copy in out_copies(d):
            copy.start()
        return carry

    lax.fori_loop(1, groups, begin, 0)
    own_copies = [
        pltpu.make_async_copy(own_in, got_in.at[me], own_sem.at[0]),
        pltpu.make_async_copy(own_up, got_up.at[me], own_sem.at[1]),
        pltpu.make_async_copy(send_gate.at[me], got_gate.at[me], own_sem.at[2]),
    ]
    for copy in own_copies:
        copy.start()

    def relay(d):
        for t in range(2):
            share(d, t, mine, far_mate, y_send, y_recv).wait_recv()
            share(d, t, theirs, core_mate, r_send, r_recv).start()

    def forward(d, carry):
        arrived = out_copies(d)
        for t in range(2):
            arrived[t].wait_recv()
            share(d, t, mine, far_mate, y_send, y_recv).start()
            share(d, t, mine, core_mate, c_send, c_recv).start()

        @pl.when(d > 1)
        def _():
            relay(d - 1)

        return carry

    lax.fori_loop(1, groups, forward, 0)
    relay(groups - 1)

    def finish(d, carry):
        for copy in out_copies(d):
            copy.wait_send()
        out_copies(d)[2].wait_recv()
        for t in range(2):
            share(d, t, mine, far_mate, y_send, y_recv).wait_send()
            share(d, t, mine, core_mate, c_send, c_recv).wait()
            share(d, t, theirs, core_mate, r_send, r_recv).wait()
        return carry

    lax.fori_loop(1, groups, finish, 0)
    for copy in own_copies:
        copy.wait()


def dispatch(groups, send_in, send_up, send_gate, own_in, own_up):
    capacity, quarter = send_in.shape[1:]
    width = own_in.shape[1]
    anywhere = pl.BlockSpec(memory_space=pl.ANY)
    dma = pltpu.SemaphoreType.DMA
    return pl.pallas_call(
        functools.partial(dispatch_kernel, groups),
        out_shape=(
            jax.ShapeDtypeStruct((groups, capacity, width), jnp.bfloat16),
            jax.ShapeDtypeStruct((groups, capacity, width), jnp.bfloat16),
            jax.ShapeDtypeStruct((groups, capacity, LANES), jnp.bfloat16),
        ),
        in_specs=[anywhere] * 5,
        out_specs=(anywhere,) * 3,
        scratch_shapes=[dma((3, groups)), dma((3, groups))]
        + [dma((2, groups))] * 6
        + [dma((3,))],
        compiler_params=pltpu.CompilerParams(collective_id=0, has_side_effects=True),
    )(send_in, send_up, send_gate, own_in, own_up)


def combine_kernel(
    groups,
    part_out,
    part_back,
    home_out,
    home_back,
    core_in,
    far_out,
    far_in,
    total,
    c_send,
    c_recv,
    y_send,
    y_recv,
    far_send,
    far_recv,
):
    me, h, core_mate, far_mate = places()
    quarter = home_out.shape[2]
    parts = (part_out, part_back)
    homes = (home_out, home_back)
    greet(groups, me, h, core_mate, far_mate)
    far_core_mate = lax.rem(core_mate + 2, 4)
    mate_quarters = (core_mate, far_core_mate)

    def owner_of(d):
        return lax.rem(me + d, groups)

    def core_copy(d, t, which):
        owner = owner_of(d)
        return pltpu.make_async_remote_copy(
            src_ref=parts[t].at[owner, :, columns(mate_quarters[which], quarter)],
            dst_ref=core_in.at[t, which, owner],
            send_sem=c_send.at[t, which, d],
            recv_sem=c_recv.at[t, which, d],
            device_id=(me, core_mate),
            device_id_type=MESH,
        )

    def far_copy(d, t):
        owner = owner_of(d)
        return pltpu.make_async_remote_copy(
            src_ref=far_out.at[t, owner],
            dst_ref=far_in.at[t, owner],
            send_sem=y_send.at[t, d],
            recv_sem=y_recv.at[t, d],
            device_id=(me, far_mate),
            device_id_type=MESH,
        )

    def home_copy(d, t):
        owner = owner_of(d)
        return pltpu.make_async_remote_copy(
            src_ref=total.at[t, owner],
            dst_ref=homes[t].at[me],
            send_sem=far_send.at[t, d],
            recv_sem=far_recv.at[t, d],
            device_id=(owner, h),
            device_id_type=MESH,
        )

    def begin(i, carry):
        d = lax.rem(i + 1, groups)
        for t in range(2):
            for which in (1, 0):
                core_copy(d, t, which).start()
        return carry

    lax.fori_loop(0, groups, begin, 0)

    def first(i):
        d = lax.rem(i + 1, groups)
        owner = owner_of(d)
        for t in range(2):
            core_copy(d, t, 1).wait_recv()
            far_out[t, owner] = (
                parts[t][owner, :, columns(far_mate, quarter)].astype(jnp.float32)
                + core_in[t, 1, owner].astype(jnp.float32)
            ).astype(jnp.bfloat16)
            far_copy(d, t).start()

    def second(i, last):
        d = lax.rem(i + 1, groups)
        owner = owner_of(d)
        for t in range(2):
            core_copy(d, t, 0).wait_recv()
            far_copy(d, t).wait_recv()
            value = (
                parts[t][owner, :, columns(h, quarter)].astype(jnp.float32)
                + core_in[t, 0, owner].astype(jnp.float32)
                + far_in[t, owner].astype(jnp.float32)
            ).astype(jnp.bfloat16)
            if last:
                homes[t][owner] = value
            else:
                total[t, owner] = value
                home_copy(d, t).start()

    first(0)

    def step(i, carry):
        first(i + 1)
        second(i, False)
        return carry

    lax.fori_loop(0, groups - 1, step, 0)
    second(groups - 1, True)

    def finish(i, carry):
        d = lax.rem(i + 1, groups)
        for t in range(2):
            for which in (0, 1):
                core_copy(d, t, which).wait_send()
            far_copy(d, t).wait_send()
        return carry

    lax.fori_loop(0, groups, finish, 0)

    def close(d, carry):
        for t in range(2):
            home_copy(d, t).wait()
        return carry

    lax.fori_loop(1, groups, close, 0)


def combine(groups, part_out, part_back):
    capacity, width = part_out.shape[1:]
    quarter = width // 4
    vmem = pl.BlockSpec(memory_space=pltpu.VMEM)
    dma = pltpu.SemaphoreType.DMA
    block = (groups, capacity, quarter)
    return pl.pallas_call(
        functools.partial(combine_kernel, groups),
        out_shape=(jax.ShapeDtypeStruct(block, jnp.bfloat16),) * 2,
        in_specs=[vmem] * 2,
        out_specs=(vmem,) * 2,
        scratch_shapes=[
            pltpu.VMEM((2, 2) + block, jnp.bfloat16),
            pltpu.VMEM((2,) + block, jnp.bfloat16),
            pltpu.VMEM((2,) + block, jnp.bfloat16),
            pltpu.VMEM((2,) + block, jnp.bfloat16),
            dma((2, 2, groups)),
            dma((2, 2, groups)),
            dma((2, groups)),
            dma((2, groups)),
            dma((2, groups)),
            dma((2, groups)),
        ],
        compiler_params=pltpu.CompilerParams(
            collective_id=1, has_side_effects=True, vmem_limit_bytes=48 * 2**20
        ),
    )(part_out, part_back)


def fused_kernel(
    groups,
    tokens,
    cotangent,
    target_col,
    target_row,
    code_row,
    threshold,
    mask,
    up_any,
    down_any,
    layer_out,
    token_grad,
    grad_up,
    grad_down,
    home_out,
    home_back,
    send_gate,
    level,
    opened,
    cross_buf,
    got_in,
    got_up,
    got_gate,
    send_buf,
    up,
    down,
    gated_all,
    dpre_all,
    part,
    core_in,
    far_out,
    far_in,
    total,
    w_sem,
    far_send,
    far_recv,
    y_send,
    y_recv,
    c_send,
    c_recv,
    r_send,
    r_recv,
    back_c_send,
    back_c_recv,
    back_y_send,
    back_y_recv,
    home_send,
    home_recv,
):
    me, h, core_mate, far_mate = places()
    quarter = home_out.shape[2]
    capacity = home_out.shape[1]
    width = tokens.shape[1]
    hidden_units = down.shape[0]
    slots = groups * capacity
    far_core_mate = lax.rem(core_mate + 2, 4)
    mate_quarters = (core_mate, far_core_mate)
    weight_copies = [
        pltpu.make_async_copy(up_any, up, w_sem.at[0]),
        pltpu.make_async_copy(down_any, down, w_sem.at[1]),
    ]
    for copy in weight_copies:
        copy.start()
    greet(groups, me, h, core_mate, far_mate)
    mine = columns(h, quarter)
    theirs = columns(far_mate, quarter)
    level[...] = threshold[...].astype(jnp.float32) / 64.0
    opened[...] = mask[...].astype(jnp.float32)
    sources = (tokens, cotangent)
    gots = (got_in, got_up)
    homes = (home_out, home_back)

    def remote(src, dst, s_sem, r_sem, device):
        return pltpu.make_async_remote_copy(
            src_ref=src,
            dst_ref=dst,
            send_sem=s_sem,
            recv_sem=r_sem,
            device_id=device,
            device_id_type=MESH,
        )

    def partner(d):
        total_bits, bit = 0, 1
        while bit < groups:
            total_bits = total_bits + lax.rem(me // bit + d // bit, 2) * bit
            bit *= 2
        return total_bits

    def owner_of(d):
        return partner(d)

    def turn(i):
        return lax.rem(5 * i, groups)

    def select(peer):
        rows = lax.broadcasted_iota(jnp.int32, (capacity, tokens.shape[0]), 0) + peer * capacity
        hits = [rows == target_row[k : k + 1, :] for k in range(target_row.shape[0])]
        gate = 0.0
        chosen = 0.0
        for k, hit in enumerate(hits):
            value = code_row[k : k + 1, :].astype(jnp.float32) / 256.0
            gate = gate + jnp.sum(jnp.where(hit, value, 0.0), axis=1, keepdims=True)
            chosen = chosen + jnp.where(hit, 1.0, 0.0)
        spread = jnp.broadcast_to(gate, (capacity, LANES)).astype(jnp.bfloat16)
        return chosen.astype(jnp.bfloat16), spread

    def out_copy(d, t):
        peer = partner(d)
        if t == 2:
            src, dst = send_gate.at[peer], got_gate.at[me]
        else:
            src, dst = send_buf.at[t, peer], gots[t].at[me, :, mine]
        return remote(src, dst, far_send.at[t, d], far_recv.at[t, d], (peer, h))

    def share(d, t, cols, mate, s_sem, r_sem):
        block = gots[t].at[owner_of(d), :, cols]
        return remote(block, block, s_sem.at[t, d], r_sem.at[t, d], (me, mate))

    def y_share(d, t):
        return share(d, t, mine, far_mate, y_send, y_recv)

    def cross_copy(t):
        return remote(
            cross_buf.at[t],
            gots[t].at[me, :, theirs],
            y_send.at[t, 1],
            y_recv.at[t, 1],
            (partner(1), h),
        )

    def core_share(d, t):
        return share(d, t, mine, core_mate, c_send, c_recv)

    def relay_share(d, t):
        return share(d, t, theirs, core_mate, r_send, r_recv)

    def core_copy(d, t, which):
        owner = owner_of(d)
        return remote(
            part.at[t, owner, :, columns(mate_quarters[which], quarter)],
            core_in.at[t, which, owner],
            back_c_send.at[t, which, d],
            back_c_recv.at[t, which, d],
            (me, core_mate),
        )

    def far_copy(d, t):
        owner = owner_of(d)
        return remote(
            far_out.at[t, owner],
            far_in.at[t, owner],
            back_y_send.at[t, d],
            back_y_recv.at[t, d],
            (me, far_mate),
        )

    def home_copy(d, t):
        owner = owner_of(d)
        return remote(
            total.at[t, owner],
            homes[t].at[me],
            home_send.at[t, d],
            home_recv.at[t, d],
            (owner, h),
        )

    def times(a, b):
        return jnp.dot(a, b, preferred_element_type=jnp.float32)

    def times_t(a, b):
        return lax.dot_general(a, b, (((1,), (1,)), ((), ())), preferred_element_type=jnp.float32)

    def t_times(a, b):
        return lax.dot_general(a, b, (((0,), (0,)), ((), ())), preferred_element_type=jnp.float32)

    def begin(i, carry):
        d = turn(i)
        peer = partner(d)
        chosen, spread = select(peer)
        send_gate[peer] = spread
        for t in range(2):
            send_buf[t, peer] = times(chosen, sources[t][:, mine]).astype(jnp.bfloat16)
            out_copy(d, t).start()
        out_copy(d, 2).start()

        @pl.when(d == 1)
        def _():
            for t in range(2):
                cross_buf[t] = times(chosen, sources[t][:, theirs]).astype(jnp.bfloat16)
                cross_copy(t).start()

        return carry

    lax.fori_loop(1, groups, begin, 0)
    own_chosen, own_spread = select(me)
    for t in range(2):
        for q in range(4):
            cols = slice(q * quarter, (q + 1) * quarter)
            gots[t][me, :, cols] = times(own_chosen, sources[t][:, cols]).astype(jnp.bfloat16)
    got_gate[me] = own_spread
    for copy in weight_copies:
        copy.wait()

    def forward(d):
        for t in range(2):
            out_copy(d, t).wait_recv()
            pl.when(d != 1)(lambda: y_share(d, t).start())
            core_share(d, t).start()

    def relay(d):
        for t in range(2):
            pl.when(d != 1)(lambda: y_share(d, t).wait_recv())
            pl.when(d == 1)(lambda: cross_copy(t).wait_recv())
            relay_share(d, t).start()

    def compute(d):
        owner = owner_of(d)
        weight_col = got_gate[owner].astype(jnp.float32)[:, :1]
        pre = times(got_in[owner], up[...])
        sigma = jax.nn.sigmoid(SHARPNESS * (pre - level[...]))
        gated = (weight_col * opened[...] * pre * sigma).astype(jnp.bfloat16)
        back_hidden = times_t(got_up[owner], down[...]) * weight_col
        slope = opened[...] * (sigma + SHARPNESS * pre * sigma * (1.0 - sigma))
        dpre = (back_hidden * slope).astype(jnp.bfloat16)
        gated_all[owner] = gated
        dpre_all[owner] = dpre
        for q in range(4):
            cols = slice(q * quarter, (q + 1) * quarter)
            part[0, owner, :, cols] = times(gated, down[:, cols]).astype(jnp.bfloat16)
            part[1, owner, :, cols] = times_t(dpre, up[cols, :]).astype(jnp.bfloat16)
        for t in range(2):
            for which in (1, 0):
                core_copy(d, t, which).start()

    def compute_arrived(d):
        for t in range(2):
            core_share(d, t).wait_recv()
            relay_share(d, t).wait_recv()
        out_copy(d, 2).wait_recv()
        compute(d)

    def first(d):
        owner = owner_of(d)
        for t in range(2):
            core_copy(d, t, 1).wait_recv()
            far_out[t, owner] = (
                part[t, owner, :, theirs].astype(jnp.float32)
                + core_in[t, 1, owner].astype(jnp.float32)
            ).astype(jnp.bfloat16)
            far_copy(d, t).start()

    def second(d):
        owner = owner_of(d)
        for t in range(2):
            core_copy(d, t, 0).wait_recv()
            far_copy(d, t).wait_recv()
            total[t, owner] = (
                part[t, owner, :, mine].astype(jnp.float32)
                + core_in[t, 0, owner].astype(jnp.float32)
                + far_in[t, owner].astype(jnp.float32)
            ).astype(jnp.bfloat16)

            @pl.when(d > 0)
            def _():
                home_copy(d, t).start()

    compute(0)

    def step(i, carry):
        pl.when(i < groups)(lambda: forward(turn(i)))
        pl.when(i == 1)(lambda: first(0))
        pl.when((i > 1) & (i <= groups))(lambda: relay(turn(i - 1)))
        pl.when(i > 3)(lambda: first(turn(i - 3)))
        pl.when(i > 3)(lambda: second(turn(i - 4)))
        pl.when((i > 2) & (i <= groups + 1))(lambda: compute_arrived(turn(i - 2)))
        return carry

    lax.fori_loop(1, groups + 3, step, 0)
    tile = 512

    def grads(left, right, result, turned):
        def one(n, carry):
            cols = columns(n, tile)
            rows = right[:, :, cols].reshape(slots, tile)
            value = t_times(left[...].reshape(slots, hidden_units), rows)
            if turned:
                result[cols, :] = value.T.astype(jnp.bfloat16)
            else:
                result[:, cols] = value.astype(jnp.bfloat16)
            return carry

        lax.fori_loop(0, width // tile, one, 0)

    grads(gated_all, got_up, grad_down, False)
    second(turn(groups - 1))
    grads(dpre_all, got_in, grad_up, True)
    for t in range(2):
        homes[t][me] = total[t, me]

    def finish(d, carry):
        for t in range(2):
            for which in (0, 1):
                core_copy(d, t, which).wait_send()
            far_copy(d, t).wait_send()

        @pl.when(d > 0)
        def _():
            for t in range(2):
                pl.when(d != 1)(lambda: y_share(d, t).wait_send())
                pl.when(d == 1)(lambda: cross_copy(t).wait_send())
                core_share(d, t).wait_send()
                relay_share(d, t).wait_send()
                home_copy(d, t).wait()
            for t in range(3):
                out_copy(d, t).wait_send()

        return carry

    lax.fori_loop(0, groups, finish, 0)
    lanes = lax.broadcasted_iota(jnp.int32, (tokens.shape[0], slots), 1)
    gather = 0.0
    for k in range(target_col.shape[1]):
        gather = gather + jnp.where(lanes == target_col[:, k : k + 1], 1.0, 0.0)
    gather = gather.astype(jnp.bfloat16)
    for home, result in ((home_out, layer_out), (home_back, token_grad)):
        result[...] = times(gather, home[...].reshape(slots, quarter)).astype(jnp.bfloat16)


def write_kernel(*refs):
    count = (len(refs) - 2) // 3
    sources, results, held = refs[:count], refs[count : 2 * count], refs[2 * count : 3 * count]
    in_sems, out_sems = refs[3 * count :]
    loads = [pltpu.make_async_copy(sources[i], held[i], in_sems.at[i]) for i in range(count)]
    stores = [pltpu.make_async_copy(held[i], results[i], out_sems.at[i]) for i in range(count)]
    for load in loads:
        load.start()
    for load, store in zip(loads, stores):
        load.wait()
        store.start()
    for store in stores:
        store.wait()


def write_out(results):
    anywhere = pl.BlockSpec(memory_space=pl.ANY)
    return pl.pallas_call(
        write_kernel,
        out_shape=tuple(jax.ShapeDtypeStruct(r.shape, r.dtype) for r in results),
        in_specs=[anywhere] * len(results),
        out_specs=(anywhere,) * len(results),
        scratch_shapes=[pltpu.VMEM(r.shape, r.dtype) for r in results]
        + [pltpu.SemaphoreType.DMA((len(results),))] * 2,
        compiler_params=pltpu.CompilerParams(vmem_limit_bytes=24 * 2**20),
    )(*results)


def fused(groups, capacity, tokens, cotangent, target, codes, threshold, mask, up_block, down_block):
    width = tokens.shape[1]
    quarter = width // 4
    hidden_units = down_block.shape[0]
    vmem = pl.BlockSpec(memory_space=pltpu.VMEM)
    anywhere = pl.BlockSpec(memory_space=pl.ANY)
    dma = pltpu.SemaphoreType.DMA
    block = (groups, capacity, quarter)
    whole = (groups, capacity, width)
    narrow = (groups, capacity, hidden_units)
    half = jnp.bfloat16
    return pl.pallas_call(
        functools.partial(fused_kernel, groups),
        out_shape=(
            jax.ShapeDtypeStruct((tokens.shape[0], quarter), half),
            jax.ShapeDtypeStruct((tokens.shape[0], quarter), half),
            jax.ShapeDtypeStruct((width, hidden_units), half),
            jax.ShapeDtypeStruct((hidden_units, width), half),
        ),
        in_specs=[vmem] * 7 + [anywhere] * 2,
        out_specs=(vmem,) * 4,
        scratch_shapes=[
            pltpu.VMEM(block, half),
            pltpu.VMEM(block, half),
            pltpu.VMEM((groups, capacity, LANES), half),
            pltpu.VMEM((1, hidden_units), jnp.float32),
            pltpu.VMEM((1, hidden_units), jnp.float32),
            pltpu.VMEM((2, capacity, quarter), half),
            pltpu.VMEM(whole, half),
            pltpu.VMEM(whole, half),
            pltpu.VMEM((groups, capacity, LANES), half),
            pltpu.VMEM((2,) + block, half),
            pltpu.VMEM((width, hidden_units), half),
            pltpu.VMEM((hidden_units, width), half),
            pltpu.VMEM(narrow, half),
            pltpu.VMEM(narrow, half),
            pltpu.VMEM((2,) + whole, half),
            pltpu.VMEM((2, 2) + block, half),
            pltpu.VMEM((2,) + block, half),
            pltpu.VMEM((2,) + block, half),
            pltpu.VMEM((2,) + block, half),
            dma((2,)),
            dma((3, groups)),
            dma((3, groups)),
        ]
        + [dma((2, groups))] * 6
        + [dma((2, 2, groups))] * 2
        + [dma((2, groups))] * 4,
        compiler_params=pltpu.CompilerParams(
            collective_id=2, has_side_effects=True, vmem_limit_bytes=58 * 2**20
        ),
    )(tokens, cotangent, target, target.T, codes.T, threshold, mask, up_block, down_block)


def expert_pass(inputs, upstream, weight_col, up_block, down_block, threshold_row, mask_row):
    pre = jnp.dot(inputs, up_block, preferred_element_type=jnp.float32)
    level = threshold_row.astype(jnp.float32) / 64.0
    opened = mask_row.astype(jnp.float32)
    sigma = jax.nn.sigmoid(SHARPNESS * (pre - level))
    gated = (weight_col * opened * pre * sigma).astype(jnp.bfloat16)
    back_hidden = (
        jnp.einsum("rd,fd->rf", upstream, down_block, preferred_element_type=jnp.float32)
        * weight_col
    )
    slope = opened * (sigma + SHARPNESS * pre * sigma * (1.0 - sigma))
    dpre = (back_hidden * slope).astype(jnp.bfloat16)
    part_out = jnp.dot(gated, down_block, preferred_element_type=jnp.float32)
    part_back = jnp.einsum("rf,df->rd", dpre, up_block, preferred_element_type=jnp.float32)
    grad_down = jnp.einsum("rf,rd->fd", gated, upstream, preferred_element_type=jnp.float32).astype(
        jnp.bfloat16
    )
    grad_up = jnp.einsum("rd,rf->df", inputs, dpre, preferred_element_type=jnp.float32).astype(
        jnp.bfloat16
    )
    return (part_out, part_back, grad_up, grad_down)


def shards(
    tokens, cotangent, expert_ids, gate_codes, up_weight, down_weight, threshold_state, spike_mask
):
    groups = lax.axis_size("expert")
    me = lax.axis_index("expert")
    h = lax.axis_index("hidden")
    tok_rows, width = tokens.shape
    quarter = width // lax.axis_size("hidden")
    top = expert_ids.shape[1]
    capacity = 4 * tok_rows // groups
    pairs = tok_rows * top
    slots = groups * capacity
    flat_ids = expert_ids.reshape(pairs)
    pair_index = jnp.arange(pairs, dtype=jnp.int32)
    earlier = (flat_ids[None, :] == flat_ids[:, None]) & (pair_index[None, :] < pair_index[:, None])
    place = jnp.sum(earlier.astype(jnp.int32), axis=1)
    target = (flat_ids * capacity + place).reshape(tok_rows, top)
    if capacity % 16 == 0 and groups & (groups - 1) == 0:
        results = fused(
            groups,
            capacity,
            tokens,
            cotangent,
            target,
            gate_codes,
            threshold_state,
            spike_mask,
            up_weight[0],
            down_weight[0],
        )
        layer_out, token_grad, grad_up, grad_down = write_out(results)
        return (layer_out, token_grad, grad_up[None], grad_down[None])
    slot_index = jnp.arange(slots, dtype=jnp.int32)
    gates = gate_codes.astype(jnp.float32) / 256.0
    hits = [target[None, :, k] == slot_index[:, None] for k in range(top)]
    pick = functools.reduce(jnp.logical_or, hits).astype(jnp.bfloat16)
    slot_gate = sum(
        jnp.sum(jnp.where(hits[k], gates[None, :, k], 0.0), axis=1) for k in range(top)
    ).astype(jnp.bfloat16)
    send_gate = jnp.broadcast_to(slot_gate[:, None], (slots, LANES)).reshape(
        groups, capacity, LANES
    )

    def choose(which, rows):
        return jnp.dot(which, rows, preferred_element_type=jnp.float32).astype(jnp.bfloat16)

    own_pick = lax.dynamic_slice_in_dim(pick, me * capacity, capacity, 0)
    tok_cut = lax.dynamic_slice_in_dim(tokens, h * quarter, quarter, 1)
    cot_cut = lax.dynamic_slice_in_dim(cotangent, h * quarter, quarter, 1)
    got_in, got_up, got_gate = dispatch(
        groups,
        choose(pick, tok_cut).reshape(groups, capacity, quarter),
        choose(pick, cot_cut).reshape(groups, capacity, quarter),
        send_gate,
        choose(own_pick, tokens),
        choose(own_pick, cotangent),
    )
    part_out, part_back, grad_up, grad_down = expert_pass(
        got_in.reshape(slots, width),
        got_up.reshape(slots, width),
        got_gate.reshape(slots, LANES)[:, :1].astype(jnp.float32),
        up_weight[0],
        down_weight[0],
        threshold_state[0],
        spike_mask[0],
    )
    home_out, home_back = combine(
        groups,
        part_out.astype(jnp.bfloat16).reshape(groups, capacity, width),
        part_back.astype(jnp.bfloat16).reshape(groups, capacity, width),
    )

    def gather_home(home):
        return jnp.einsum(
            "st,sw->tw", pick, home.reshape(slots, quarter), preferred_element_type=jnp.float32
        ).astype(jnp.bfloat16)

    return (gather_home(home_out), gather_home(home_back), grad_up[None], grad_down[None])


def solution(mesh):
    placed = (
        P("expert", None),
        P("expert", None),
        P("expert", None),
        P("expert", None),
        P("expert", None, "hidden"),
        P("expert", "hidden", None),
        P("expert", "hidden"),
        P("expert", "hidden"),
    )
    return jax.shard_map(
        shards,
        mesh=mesh,
        in_specs=placed,
        out_specs=(
            P("expert", "hidden"),
            P("expert", "hidden"),
            P("expert", None, "hidden"),
            P("expert", "hidden", None),
        ),
        check_vma=False,
    )
```
